32 devices in a mesh: face: 2 (over x), rows: 16 (over z, y, core).
Axes of the slice: x: 2, y: 2, z: 4, core: 2. Of those that a mesh axis runs over, the one named last changes fastest.
Arguments:
- final_adjoint: float32 [16, 6, 256, 256], P(None, 'face', 'rows'), may hold values from -6 to 6
- courant_x: float32 [16, 6, 256, 256], P(None, 'face', 'rows'), may hold values from 0.05 to 0.45
- courant_y: float32 [16, 6, 256, 256], P(None, 'face', 'rows'), may hold values from 0.05 to 0.45
- ray_tiles: bfloat16 [2, 1024, 16, 512], P('face', 'rows'), may hold values from -1.5 to 1.5
- ray_innov: bfloat16 [2, 1024, 16], P('face', 'rows'), may hold values from -6 to 6
- ray_dest: int32 [2, 1024, 1], P('face', 'rows'), may hold values from 0 to 15; in each aligned block of 64 rows (0 to 63, 64 to 127, ..., all dimensions but the last counted through in order) at most 8 rows name the same one
- ray_cols: int32 [2, 1024, 32], P('face', 'rows'), may hold values from 0 to 12287
Outputs:
- prior_adjoint: float32 [16, 6, 256, 256], P(None, 'face', 'rows')
The draws below stay inside these ranges and needn't reach their ends.
Inputs may be any that keep to these rules, and one draw needn't show every extreme that they name: `ray_dest`: each device's 64 ray blocks name one band each, at most 8 blocks for one band; some device sends exactly 8 blocks to some band.
All inputs are finite; a program needn't handle non-finite values.
Results may differ from the reference program's by a relative error of at most 0.0003.
Values may be sent and summed in bfloat16 or wider, within the bound.
No kernel may reach another device: no remote copies, remote signals or barrier semaphores. Data moves between devices by JAX's collectives and lax.ppermute only.
A program may use at most 128 MiB of HBM per device.

```python
import math
import jax
import jax.numpy as jnp
import numpy as np

FACES = 6
LEV = 16
RD = 16
RAYS = 16
K = 32
BLK_DEV = 64
BANDS = 16
NC = 256
CAP = 8
N_FACE = 2


def set_ends(values, rng, smallest, largest):
    longest = values.shape.index(max(values.shape))
    spots = []
    for shift in (0, 1):
        where = [jax.random.randint(jax.random.fold_in(rng, axis), (), 0, length) for axis, length in enumerate(values.shape)]
        where[longest] = (where[longest] + shift) % values.shape[longest]
        spots.append(tuple(where))
    return values.at[spots[0]].set(smallest).at[spots[1]].set(largest)


def shard_levels(stream_key, shape, pieces, least, largest):
    level = 1.0
    for axis_at, blocks in pieces:
        steps = jax.random.uniform(jax.random.fold_in(jax.random.fold_in(stream_key, 6), axis_at), (blocks,), jnp.float32, least / len(pieces), largest / len(pieces))
        level = level * jnp.repeat(jnp.exp(steps), shape[axis_at] // blocks).reshape((-1,) + (1,) * (len(shape) - 1 - axis_at))
    return level


def shared_out(key, own, number, rows, number_of, top, most, lean):
    order = jax.random.permutation(key, number_of)
    packed, common = load_shares(number_of, rows * top, most, lean, True), load_shares(number_of, rows * top, most, lean, False)
    places = jnp.arange(number_of)

    def named(tallies, turn):
        used = int((tallies > 0).sum())
        fixed = max(1, used // 4)
        shifted = fixed + (places - fixed + turn * (used - fixed)) % max(1, number_of - fixed)
        return jnp.zeros((number_of,), jnp.int32).at[order[jnp.where(places < fixed, places, shifted)]].set(jnp.asarray(tallies, jnp.int32))

    tallies = jnp.where(number % 4 == 0, named(packed, number // 4), named(common, number - number // 4 - 1))
    mixed = jax.random.permutation(jax.random.fold_in(own, 3), number_of)
    source_of, taker = mixed[0:number_of // 2 * 2:2], mixed[1:number_of // 2 * 2:2]
    slack = jnp.minimum(tallies[source_of] - 1, most - tallies[taker]) // 2
    slack = jnp.where((source_of == order[0]) | (taker == order[0]) | (tallies[taker] == 0), 0, jnp.maximum(slack, 0))
    shifted = jax.random.randint(jax.random.fold_in(own, 4), (number_of // 2,), 0, 1 << 20) % (slack + 1)
    tallies = tallies.at[source_of].add(-shifted).at[taker].add(shifted)
    members = jnp.searchsorted(jnp.cumsum(tallies), jnp.arange(rows * top), side="right").astype(jnp.int32)
    table = members.reshape(top, rows).T
    table = table[jax.random.permutation(jax.random.fold_in(own, 1), rows)]
    turn = jax.random.randint(jax.random.fold_in(own, 2), (rows, 1), 0, top)
    return jnp.take_along_axis(table, (jnp.arange(top)[None, :] + turn) % top, axis=1)


def load_shares(count, total, limit, slope, full):
    loads = [(1 << 20) // math.isqrt(standing ** slope) + 1 for standing in range(1, count + 1)]
    largest = limit if full else min(limit, max(-(-total // count), total * loads[0] // sum(loads)))
    least = 1 if total - largest >= count - 1 else 0
    holding, surplus = [largest] + [least] * (count - 1), total - largest - least * (count - 1)
    while surplus > 0:
        free = [i for i in range(1, count) if holding[i] < largest] or [i for i in range(1, count) if holding[i] < limit]
        pool, left = sum([loads[i] for i in free]), surplus
        for i in free:
            addition = min(limit - holding[i], max(1, left * loads[i] // pool), surplus)
            holding[i] = holding[i] + addition
            surplus = surplus - addition
    return np.array(holding)


def normal_values(own_key, shape, width, bound, pieces=(), held_as=jnp.bfloat16):
    array = jax.random.normal(own_key, shape, jnp.float32) * width
    if len(pieces) > 0:
        array = shard_levels(own_key, shape, pieces, -0.22, 0.18) * array
    return jnp.clip(array, min=-bound, max=bound).astype(held_as)


def setup_inputs(seed: int = 0) -> dict:
    splits = jax.random.split(jax.random.key(seed), 8)
    final_adjoint = normal_values(splits[0], (LEV, FACES, NC, NC), 1.0, 6.0, ((1, 2), (2, 16)), jnp.float32)
    courant_x = jnp.clip(0.05 + 0.39999999 * jax.random.uniform(splits[1], (LEV, FACES, NC, NC), jnp.float32) ** shard_levels(splits[1], (LEV, FACES, NC, NC), ((1, 2), (2, 16)), -0.2, 0.2), 0.05, 0.45)
    courant_y = jnp.clip(0.05 + 0.39999999 * jax.random.uniform(splits[2], (LEV, FACES, NC, NC), jnp.float32) ** shard_levels(splits[2], (LEV, FACES, NC, NC), ((1, 2), (2, 16)), -0.2, 0.2), 0.05, 0.45)
    ray_tiles = normal_values(splits[3], (N_FACE, BANDS * BLK_DEV, RAYS, LEV * K), RAYS ** -0.5, 1.5, ((0, 2), (1, 16)))
    ray_innov = normal_values(splits[4], (N_FACE, BANDS * BLK_DEV, RAYS), 1.0, 6.0, ((0, 2), (1, 16)))
    ray_dest_keys = jax.random.split(jax.random.fold_in(splits[5], 1), N_FACE * (BANDS * BLK_DEV) // BLK_DEV)
    ray_dest_turns = jax.random.permutation(jax.random.fold_in(splits[5], 3), N_FACE * (BANDS * BLK_DEV) // BLK_DEV)
    ray_dest = jax.vmap(lambda own, number: shared_out(jax.random.fold_in(splits[5], 2), own, number, BLK_DEV, BANDS, 1, CAP, 2))(ray_dest_keys, ray_dest_turns).reshape((N_FACE, BANDS * BLK_DEV, 1))
    ray_cols = set_ends(jax.random.randint(splits[6], (N_FACE, BANDS * BLK_DEV, K), 0, 3 * RD * NC), jax.random.fold_in(splits[6], 1), 0, (3 * RD * NC) - 1).astype(jnp.int32)
    return dict(final_adjoint=final_adjoint, courant_x=courant_x, courant_y=courant_y, ray_tiles=ray_tiles, ray_innov=ray_innov, ray_dest=ray_dest, ray_cols=ray_cols)


def forward(field, courant_x, courant_y):
    left_ghost = jnp.roll(field[..., -1], 1, axis=1)
    rotated = field[:, :, ::-1, 0]
    straight = field[:, :, -1, :]
    ghosts = []
    for face_no in range(FACES):
        if face_no % 2 == 0:
            ghosts.append(rotated[:, (face_no + 2) % FACES])
        else:
            ghosts.append(straight[:, (face_no + 1) % FACES])
    top_ghost = jnp.stack(ghosts, axis=1)
    west = jnp.concatenate([left_ghost[..., None], field[..., :-1]], axis=-1)
    north = jnp.concatenate([top_ghost[:, :, None, :], field[:, :, :-1, :]], axis=2)
    return (1.0 - courant_x - courant_y) * field + courant_x * west + courant_y * north

def transpose_step(adjoint, courant_x, courant_y):
    zeros = jnp.zeros_like(adjoint)
    _, pullback = jax.vjp(lambda v: forward(v, courant_x, courant_y), zeros)
    return pullback(adjoint)[0]

def reference(final_adjoint, courant_x, courant_y, ray_tiles, ray_innov, ray_dest, ray_cols):
    contrib = jnp.einsum('gnr,gnrk->gnk', ray_innov.astype(jnp.float32), ray_tiles.astype(jnp.float32))
    groups, blocks = (contrib.shape[0], contrib.shape[1])
    contrib = contrib.reshape(groups, blocks, LEV, K)
    per_group = FACES // N_FACE
    group_id = jnp.arange(groups, dtype=jnp.int32)[:, None, None]
    face_id = per_group * group_id + ray_cols // (RD * NC)
    row_id = ray_dest[..., 0:1] * RD + ray_cols // NC % RD
    col_id = ray_cols % NC
    flat_id = (face_id * NC * NC + row_id * NC + col_id).astype(jnp.int32)
    values = jnp.transpose(contrib, (2, 0, 1, 3)).reshape(LEV, -1)
    forcing = jnp.zeros((LEV, FACES * NC * NC), jnp.float32).at[:, flat_id.reshape(-1)].add(values)
    forcing = forcing.reshape(LEV, FACES, NC, NC)
    mid_adjoint = transpose_step(final_adjoint, courant_x, courant_y) + forcing
    return transpose_step(mid_adjoint, courant_x, courant_y)
```

```python
import functools

import jax
import jax.numpy as jnp
from jax import lax
from jax.experimental import pallas as pl
from jax.experimental.pallas import tpu as pltpu
from jax.sharding import PartitionSpec as P


LOW = 4
KINDS = 8
VMEM = pl.BlockSpec(memory_space=pltpu.VMEM)
f32, bf16, i32 = jnp.float32, jnp.bfloat16, jnp.int32


def iota(shape, dim):
    return lax.broadcasted_iota(i32, shape, dim)


def spot():
    return lax.axis_index("face") == 0, lax.axis_index("rows")


def mm(x, y, dims=((1,), (0,))):
    return lax.dot_general(x, y, (dims, ((), ())), preferred_element_type=f32)


def halves(value):
    high = value.astype(bf16)
    return high, (value - high.astype(f32)).astype(bf16)


def level_code(top):
    return jnp.floor(16.0 * jnp.log2(jnp.maximum(top, 1e-30)) + 1.25)


def quantized(value, code):
    return jnp.floor(value * (32767.0 * jnp.exp2(code * (-1.0 / 16.0))) + 0.5).astype(i32)


def step_size(code):
    return jnp.exp2(code * (1.0 / 16.0)) * (1.0 / 32767.0)


def pair(first, second):
    return lax.shift_left(first, 16) | (second & 0xFFFF)


def upper(packed):
    return lax.shift_right_arithmetic(packed, 16).astype(f32)


def lower(packed):
    return lax.shift_right_arithmetic(lax.shift_left(packed, 16), 16).astype(f32)


def to_rows(line, base, band, flip):
    shape = (band, line.shape[1])
    row = iota(shape, 0)
    want = base + (band - 1 - row if flip else row)
    return jnp.sum(jnp.where(iota(shape, 1) == want, line, 0.0), axis=1, keepdims=True)


def to_lanes(column, base, width):
    shape = (column.shape[0], width)
    return jnp.sum(jnp.where(iota(shape, 1) == iota(shape, 0) + base, column, 0.0), axis=0, keepdims=True)


def edge_kernel(a, cx, cy, out):
    first, _ = spot()
    levels, _, _, edge = a.shape
    band = cx.shape[2]
    row = [a[:, f, 0, :] * cy[:, f, 0, :] for f in (1, 2)]
    out[:, :edge] = jnp.where(first, row[1], row[0])
    for level in range(levels):
        column = (a[level, 0] * cx[level, 0])[:, 0:1]
        out[level : level + 1, edge : edge + 128] = to_lanes(column, 0, 128)


def contrib_kernel(slots, tiles, innov, dest, cells, contrib, where_, crown):
    blocks, rays = innov.shape
    width = cells.shape[1]
    total = tiles.shape[1]
    levels = total // width
    _, band_id = spot()
    bands = contrib.shape[0] // slots
    high = bands // LOW
    square = (blocks, blocks)
    target = dest[...]
    across = jnp.sum(jnp.where(iota(square, 0) == iota(square, 1), target, 0), axis=0, keepdims=True)
    earlier = (across == target) & (iota(square, 1) < iota(square, 0))
    order = jnp.sum(jnp.where(earlier, 1, 0), axis=1, keepdims=True)
    apart = target ^ band_id
    slot = ((apart & (LOW - 1)) * high + apart // LOW) * slots + order
    slot = jnp.sum(jnp.where(iota(square, 0) == iota(square, 1), slot, 0), axis=0, keepdims=True)
    rows = contrib.shape[0]
    pick = (iota((rows, blocks), 0) == slot).astype(f32).astype(bf16)
    long = blocks * rays
    repeat = (iota((rays, long), 1) % rays == iota((rays, long), 0)).astype(f32).astype(bf16)
    spread = mm(innov[...], repeat)
    spread = jnp.where(iota((blocks, long), 1) // rays == iota((blocks, long), 0), spread, 0.0)
    weights = mm(pick, spread.astype(bf16)).astype(bf16)
    sums = mm(weights, tiles[...])
    contrib[...] = sums
    place = (iota((width, 128), 0) == iota((width, 128), 1)).astype(f32).astype(bf16)
    byte = [mm(pick, mm(part.astype(f32).astype(bf16), place).astype(bf16)) for part in (cells[...] // 256, cells[...] % 256)]
    chosen = byte[0] * 256.0 + byte[1]
    where_[...] = chosen.astype(i32)

    edge = crown.shape[2]
    first, _ = spot()
    begin = ((band_id & (LOW - 1)) * high + band_id // LOW) * slots
    mine = (iota((slots, blocks), 0) + begin == slot).astype(f32).astype(bf16)
    near = mm(mm(mine, spread.astype(bf16)).astype(bf16), tiles[...])
    stack = jnp.concatenate([jnp.broadcast_to(near[j : j + 1], (levels, total)) for j in range(slots)], axis=0)
    tall = slots * levels
    stack = jnp.where(iota((tall, total), 1) // width == iota((tall, total), 0) % levels, stack, 0.0)
    count = slots * width
    fold = (iota((total, count), 0) % width == iota((total, count), 1) % width).astype(f32).astype(bf16)
    parts = halves(stack)
    wide = mm(parts[0], fold) + mm(parts[1], fold)
    wide = jnp.where(iota((tall, count), 1) // width == iota((tall, count), 0) // levels, wide, 0.0)
    entry = sum(wide[j * levels : (j + 1) * levels] for j in range(slots))
    tile = (iota((width, count), 0) == iota((width, count), 1) % width).astype(f32).astype(bf16)
    byte = [mm(mm(mine, part.astype(f32).astype(bf16)).astype(bf16), tile) for part in (cells[...] // 256, cells[...] % 256)]
    spots = byte[0] * 256.0 + byte[1]
    spots = jnp.where(iota((slots, count), 1) // width == iota((slots, count), 0), spots, 0.0)
    spots = jnp.sum(spots, axis=0, keepdims=True).astype(i32)
    line, column = spots // edge, spots % edge
    band = 16
    chart = (iota((edge, count), 0) == column).astype(f32).astype(bf16)
    rows_of = (0, jnp.where(first, 2 * band, band))
    picked = jnp.concatenate([jnp.where(line == r, entry, 0.0) for r in rows_of], axis=0)
    parts = halves(picked)
    both = ((1,), (1,))
    result = mm(parts[0], chart, both) + mm(parts[1], chart, both)
    crown[0] = result[:levels]
    crown[1] = result[levels:]


def pack_kernel(slots, contrib, where_, crown, a, cx, cy, traded, *refs):
    sends, below, hold = refs[:LOW], refs[LOW], refs[LOW + 1]
    levels, faces, _, edge = a.shape
    first, band_id = spot()
    bands = contrib.shape[0] // slots
    high = bands // LOW
    band = edge // bands
    for f in range(faces):
        below[:, f, :] = a[:, f, 0, :] * cy[:, f, 0, :]

    def row(ref, f, r):
        return ref[:, f, r, :]

    def out_row(ref, r):
        return jnp.where(first, row(ref, 2, r), row(ref, 1, r))

    lane = iota((levels, edge), 1)
    cross = traded[:, :edge]
    side0 = traded[:, edge : edge + 1]

    def top(get, right, left):
        a0, x0, y0 = get(a, 0), get(cx, 0), get(cy, 0)
        flow = pltpu.roll(x0 * a0, edge - 1, 1)
        flow = jnp.where(lane == edge - 1, right, flow)
        mid = (1.0 - x0 - y0) * a0 + flow + get(a, 1) * get(cy, 1)
        mid = mid + jnp.where(lane == 0, left, 0.0)
        return y0 * a0, y0, y0 * mid

    corner = [(a[:, f, 0, 0:1] * cx[:, f, 0, 0:1]) for f in (1, 2)]
    u_loc, y_loc, q_loc = top(lambda ref, r: row(ref, 0, r), corner[0], cross[:, edge - 1 :])
    u_out, y_out, q_out = top(
        out_row,
        jnp.where(first, side0, corner[1]),
        jnp.where(first, u_loc[:, edge - 1 :], cross[:, edge - 1 :]),
    )
    source = band_id == 0
    local = source & first
    kinds = [crown[0], crown[1]]
    kinds += [jnp.where(ok, v, 0.0) for ok, v in ((local, u_loc), (source, cross), (local, y_loc), (source, y_out), (local, q_loc), (source, q_out))]
    slim = iota((levels, 128), 1) // band
    code = jnp.zeros((1, 128), f32)
    for n, kind in enumerate(kinds):
        peak = jnp.max(jnp.max(jnp.abs(kind), axis=1, keepdims=True), axis=0, keepdims=True)
        code = jnp.where(slim[:1] == n, level_code(peak), code)
    for b in range(bands):
        low_at = edge - band * (b + 1)
        half, off = low_at // 128, low_at % 128
        tile = jnp.zeros((levels, 128), f32)
        for n, kind in enumerate(kinds):
            part = kind[:, half * 128 : half * 128 + 128]
            move = (n * band - off) % 128
            tile = jnp.where(slim == n, pltpu.roll(part, move, 1) if move else part, tile)
        q = quantized(tile, code)
        hold[b] = pair(q[: levels // 2], q[levels // 2 :])

    code_rows = code.astype(i32)
    n = high * slots
    total = contrib.shape[1]
    half = total // 2
    quarter = half // 2
    for k in range(LOW):
        out = sends[k]
        block = contrib[k * n : (k + 1) * n, :]
        codes = []
        for h in range(2):
            values = block[:, h * half : (h + 1) * half]
            c = level_code(jnp.max(jnp.abs(values), axis=1, keepdims=True))
            q = quantized(values, c)
            out[h * n : (h + 1) * n, :] = pair(q[:, :quarter], q[:, quarter:])
            codes.append(c.astype(i32))
        tag = where_[k * n : (k + 1) * n, :]
        width = total // levels
        column, slot = iota((n, 128), 1), iota((n, 128), 0) % slots
        tag = jnp.where(column == width, codes[0], tag)
        tag = jnp.where(column == width + 1, codes[1], tag)
        tag = jnp.where((column >= 64) & (slot == 0), pltpu.roll(code_rows, 64, 1), tag)
        tag = jnp.where((column >= 64) & (slot == 1), code_rows, tag)
        out[2 * n : 3 * n, :] = tag
        for m in range(high):
            out[3 * n + KINDS * m : 3 * n + KINDS * (m + 1), :] = hold[band_id ^ (m * LOW + k)]


def regroup_kernel(slots, high, *refs):
    got, sends = refs[:LOW], refs[LOW:]
    n, w = high * slots, LOW * slots
    for m in range(high):
        for k in range(LOW):
            for part in range(3):
                sends[m][part * w + k * slots : part * w + (k + 1) * slots, :] = got[k][part * n + m * slots : part * n + (m + 1) * slots, :]
            sends[m][3 * w + KINDS * k : 3 * w + KINDS * (k + 1), :] = got[k][3 * n + KINDS * m : 3 * n + KINDS * (m + 1), :]


def step_level(field, x, y, last_column, last_row):
    faces = len(field)
    band, edge = field[0].shape
    along = [x[f] * field[f] for f in range(faces)]
    upward = [y[f] * field[f] for f in range(faces)]
    shape = (band, edge)
    at_right, at_bottom = iota(shape, 1) == edge - 1, iota(shape, 0) == band - 1
    outs = []
    for f in range(faces):
        flow = pltpu.roll(along[f], edge - 1, 1)
        column = along[f + 1][:, 0:1] if f < faces - 1 else last_column
        flow = jnp.where(at_right, column, flow)
        lift = pltpu.roll(upward[f], band - 1, 0)
        lift = jnp.where(at_bottom, last_row[f], lift)
        outs.append((1.0 - x[f] - y[f]) * field[f] + flow + lift)
    return outs


def bottom_rows(level, first, last, below, unrot):
    got = [below[level, f : f + 1, :] for f in range(3)]
    far = unrot[level : level + 1, :]
    zero = jnp.zeros_like(got[0])
    seam = (
        jnp.where(first, far, zero),
        jnp.where(first, zero, got[0]),
        jnp.where(first, got[1], zero),
    )
    return [jnp.where(last, s, g) for s, g in zip(seam, got)]


def mid_kernel(a, cx, cy, below, unrot, traded, mid):
    levels, faces, band, edge = a.shape
    first, band_id = spot()
    last = band_id == lax.axis_size("rows") - 1

    def body(level, carry):
        column = to_rows(traded[level : level + 1, edge : edge + 128], 0, band, False)
        rows = bottom_rows(level, first, last, below, unrot)
        outs = step_level([a[level, f] for f in range(faces)], cx[level], cy[level], column, rows)
        for f in range(faces):
            mid[level, f] = outs[f]
        return carry

    for level in range(levels):
        body(level, 0)


def force_kernel(slots, width, high, *refs):
    got = refs[:high]
    mid, cx, cy = refs[high : high + 3]
    result, below, trade = refs[high + 3 : high + 6]
    flat, where_, charts, lines, field, seams = refs[high + 6 :]
    levels, faces, band, edge = mid.shape
    first, _ = spot()
    w = LOW * slots
    total = high * w
    per = 128 // width
    tags = jnp.concatenate([ref[2 * w : 3 * w, :] for ref in got], axis=0)
    for h in range(2):
        packed = jnp.concatenate([ref[h * w : (h + 1) * w, :] for ref in got], axis=0)
        size = step_size(tags[:, width + h : width + h + 1].astype(f32))
        flat[h * 256 : h * 256 + 128, :] = jnp.transpose(upper(packed) * size)
        flat[h * 256 + 128 : h * 256 + 256, :] = jnp.transpose(lower(packed) * size)
    where_[...] = jnp.transpose(tags.astype(f32))[:width]
    seam = jnp.zeros((levels, 128), f32)
    slim = iota((1, 128), 1)
    for ref in got:
        for k in range(LOW):
            tag = ref[2 * w + k * slots : 2 * w + k * slots + 2, :]
            code = jnp.where(slim < 64, pltpu.roll(tag[0:1], 64, 1), tag[1:2]).astype(f32)
            piece = ref[3 * w + KINDS * k : 3 * w + KINDS * (k + 1), :]
            seam = seam + jnp.concatenate([upper(piece), lower(piece)], axis=0) * step_size(code)
    again = pltpu.roll(seam, 128 - 6 * band, 1) + pltpu.roll(seam, 128 - 4 * band, 1) * seam
    spots = where_[...].astype(i32)
    line, column = spots // edge, spots % edge
    for k in range(width):
        charts[:, k * total : (k + 1) * total] = (iota((edge, total), 0) == column[k : k + 1]).astype(f32).astype(bf16)
    both = ((1,), (1,))
    rest = faces * levels * band
    for f in range(faces):
        hit = [(iota((band, total), 0) + f * band == line[k : k + 1]).astype(f32) for k in range(width)]

        def fill(level, carry, f=f, hit=hit):
            at = pl.multiple_of((f * levels + level) * band, band)
            for k in range(width):
                high_, low_ = halves(flat[pl.ds(level * width + k, 1), :])
                lines[pl.ds(at, band), k * total : (k + 1) * total] = (hit[k] * high_.astype(f32)).astype(bf16)
                lines[pl.ds(at + rest, band), k * total : (k + 1) * total] = (hit[k] * low_.astype(f32)).astype(bf16)
            return carry

        lax.fori_loop(0, levels, fill, 0)
    field[...] = mm(lines[...], charts[...], both)
    shape = (band, edge)
    at_left = iota(shape, 1) == 0
    zero_column = jnp.zeros((band, 1), f32)
    zero_row = jnp.zeros((1, edge), f32)
    seams[0] = seam
    seams[1] = again
    spot_ = iota((1, 128), 1)

    def body(level, carry):
        now, later = seams[0, level : level + 1, :], seams[1, level : level + 1, :]
        local = to_rows(now, 2 * band, band, True)
        cross = to_rows(now, 3 * band, band, True)
        columns = (jnp.where(first, cross, 0.0), jnp.where(first, 0.0, cross), local)
        faces_now = []
        for f in range(faces):
            at = (f * levels + level) * band
            value = mid[level, f] + field[at : at + band, :] + field[at + rest : at + rest + band, :]
            faces_now.append(value + jnp.where(at_left, columns[f], 0.0))
        outs = step_level(faces_now, cx[level], cy[level], zero_column, [zero_row] * faces)
        outs[2] = outs[2] + jnp.where(at_left, to_rows(later, 0, band, True), 0.0)
        for f in range(faces):
            result[level, f] = outs[f]
            below[level : level + 1, f : f + 1, :] = (faces_now[f][0:1] * cy[level, f, 0:1, :])[None]
        side = to_lanes((faces_now[0] * cx[level, 0])[:, 0:1], 0, 128)
        trade[level : level + 1, :] = jnp.where(spot_ < band, side, jnp.where(spot_ < 2 * band, later, 0.0))
        return carry

    for level in range(levels):
        body(level, 0)


def final_kernel(part, below, unrot, traded, out):
    levels, faces, band, edge = part.shape
    first, band_id = spot()
    last = band_id == lax.axis_size("rows") - 1
    shape = (band, edge)
    at_left, at_right, at_bottom = iota(shape, 1) == 0, iota(shape, 1) == edge - 1, iota(shape, 0) == band - 1

    def body(level, carry):
        line = traded[level : level + 1, :]
        side = to_rows(line, 0, band, False)
        cross = to_rows(line, band, band, True)
        rows = bottom_rows(level, first, last, below, unrot)
        columns = (jnp.where(first, cross, 0.0), jnp.where(first, 0.0, cross))
        for f in range(faces):
            value = part[level, f] + jnp.where(at_bottom, rows[f], 0.0)
            if f < 2:
                value = value + jnp.where(at_left, columns[f], 0.0)
            else:
                value = value + jnp.where(at_right, side, 0.0)
            out[level, f] = value
        return carry

    for level in range(levels):
        body(level, 0)


def call(kernel, outs, args, scratch=(), specs=None):
    return pl.pallas_call(
        kernel,
        out_shape=outs,
        in_specs=specs or [VMEM] * len(args),
        out_specs=jax.tree.map(lambda _: VMEM, outs),
        scratch_shapes=scratch,
        grid=(1,) if specs else (),
    )(*args)


def shape(dims, kind=f32):
    return jax.ShapeDtypeStruct(dims, kind)


def strip(levels, faces, rows, edge):
    return pl.BlockSpec((levels, faces, rows, edge), lambda _: (0, 0, 0, 0))


def exchange(value, apart):
    count = lax.axis_size("rows")
    return lax.ppermute(value, "rows", [(i, i ^ apart) for i in range(count)])


def shift_up(value):
    count = lax.axis_size("rows")
    return lax.ppermute(value, "rows", [(i, (i + count - 1) % count) for i in range(count)])


def swap_faces(value):
    return lax.ppermute(value, "face", [(0, 1), (1, 0)])


def seam_jump(value):
    count = lax.axis_size("rows")
    return lax.ppermute(value, ("face", "rows"), [(count, count - 1)])


def per_device(final_adjoint, courant_x, courant_y, ray_tiles, ray_innov, ray_dest, ray_cols):
    a, cx, cy = final_adjoint, courant_x, courant_y
    levels, faces, band, edge = a.shape
    bands = lax.axis_size("rows")
    blocks, rays, total = ray_tiles.shape[1:]
    width = ray_cols.shape[2]
    slots = max(2, 2 * blocks // bands)
    high = bands // LOW
    top = strip(levels, faces, 8, edge)
    early = call(edge_kernel, shape((levels, edge + 128)), (a, cx, cy))
    traded = swap_faces(early)
    contrib, where_, crown = call(
        functools.partial(contrib_kernel, slots),
        (shape((bands * slots, total)), shape((bands * slots, 128), i32), shape((2, levels, edge))),
        (ray_tiles[0].reshape(blocks * rays, total), ray_innov[0], ray_dest[0], ray_cols[0]),
    )
    rows = high * (3 * slots + KINDS)
    packed = call(
        functools.partial(pack_kernel, slots),
        (shape((rows, 128), i32),) * LOW + (shape((levels, faces, edge)),),
        (contrib, where_, crown, a, cx, cy, traded),
        scratch=[pltpu.VMEM((bands, KINDS, 128), i32)],
        specs=[VMEM] * 3 + [top] * 3 + [VMEM],
    )
    got = [packed[0]] + [exchange(packed[k], k) for k in range(1, LOW)]
    below = packed[LOW]
    sends = call(
        functools.partial(regroup_kernel, slots, high),
        (shape((LOW * (3 * slots + KINDS), 128), i32),) * high,
        got,
    )
    below_got = shift_up(below)
    unrot_got = seam_jump(below[:, 2])
    arrived = [sends[0]] + [exchange(sends[m], m * LOW) for m in range(1, high)]
    mid = call(mid_kernel, shape(a.shape), (a, cx, cy, below_got, unrot_got, traded))
    count = bands * slots
    part, below, trade = call(
        functools.partial(force_kernel, slots, width, high),
        (shape(a.shape), shape((levels, faces, edge)), shape((levels, 128))),
        (*arrived, mid, cx, cy),
        scratch=[
            pltpu.VMEM((total, count), f32),
            pltpu.VMEM((width, count), f32),
            pltpu.VMEM((edge, width * count), bf16),
            pltpu.VMEM((2 * levels * faces * band, width * count), bf16),
            pltpu.VMEM((2 * levels * faces * band, edge), f32),
            pltpu.VMEM((2, levels, 128), f32),
        ],
    )
    below_got = shift_up(below)
    unrot_got = seam_jump(below[:, 2])
    trade_got = swap_faces(trade)
    return call(final_kernel, shape(a.shape), (part, below_got, unrot_got, trade_got))


def solution(mesh):
    placed = (
        P(None, "face", "rows", None),
        P(None, "face", "rows", None),
        P(None, "face", "rows", None),
        P("face", "rows", None, None),
        P("face", "rows", None),
        P("face", "rows", None),
        P("face", "rows", None),
    )
    return jax.shard_map(
        per_device,
        mesh=mesh,
        in_specs=placed,
        out_specs=P(None, "face", "rows", None),
        check_vma=False,
    )
```

```python
import functools

import jax
import jax.numpy as jnp
from jax import lax
from jax.experimental import pallas as pl
from jax.experimental.pallas import tpu as pltpu
from jax.sharding import PartitionSpec as P


LOW = 4
KINDS = 8
VMEM = pl.BlockSpec(memory_space=pltpu.VMEM)
f32, bf16, i32 = jnp.float32, jnp.bfloat16, jnp.int32


def iota(shape, dim):
    return lax.broadcasted_iota(i32, shape, dim)


def spot():
    return lax.axis_index("face") == 0, lax.axis_index("rows")


def mm(x, y, dims=((1,), (0,))):
    return lax.dot_general(x, y, (dims, ((), ())), preferred_element_type=f32)


def halves(value):
    high = value.astype(bf16)
    return high, (value - high.astype(f32)).astype(bf16)


def level_code(top):
    return jnp.floor(16.0 * jnp.log2(jnp.maximum(top, 1e-30)) + 1.25)


def quantized(value, code):
    return jnp.floor(value * (32767.0 * jnp.exp2(code * (-1.0 / 16.0))) + 0.5).astype(i32)


def step_size(code):
    return jnp.exp2(code * (1.0 / 16.0)) * (1.0 / 32767.0)


def pair(first, second):
    return lax.shift_left(first, 16) | (second & 0xFFFF)


def upper(packed):
    return lax.shift_right_arithmetic(packed, 16).astype(f32)


def lower(packed):
    return lax.shift_right_arithmetic(lax.shift_left(packed, 16), 16).astype(f32)


def to_rows(line, base, band, flip):
    shape = (band, line.shape[1])
    row = iota(shape, 0)
    want = base + (band - 1 - row if flip else row)
    return jnp.sum(jnp.where(iota(shape, 1) == want, line, 0.0), axis=1, keepdims=True)


def to_lanes(column, base, width):
    shape = (column.shape[0], width)
    return jnp.sum(jnp.where(iota(shape, 1) == iota(shape, 0) + base, column, 0.0), axis=0, keepdims=True)


def edge_kernel(a, x, y, out, a_top, y_top, a_left, x_left, arrived):
    first, _ = spot()
    levels, edge = a.shape[0], a.shape[3]
    copies = [
        pltpu.make_async_copy(a.at[:, :, 0:8, :], a_top, arrived.at[0]),
        pltpu.make_async_copy(y.at[:, :, 0:8, :], y_top, arrived.at[1]),
        pltpu.make_async_copy(a.at[:, 0, :, 0:128], a_left, arrived.at[2]),
        pltpu.make_async_copy(x.at[:, 0, :, 0:128], x_left, arrived.at[3]),
    ]
    for copy in copies:
        copy.start()
    for copy in copies:
        copy.wait()
    row = [a_top[:, f, 0, :] * y_top[:, f, 0, :] for f in (1, 2)]
    out[:, :edge] = jnp.where(first, row[1], row[0])
    out[:, edge : 2 * edge] = row[1]
    for level in range(levels):
        column = (a_left[level] * x_left[level])[:, 0:1]
        out[level : level + 1, 2 * edge :] = to_lanes(column, 0, 128)


def fold(value):
    q = value.shape[0] // 4
    group = iota((q, 128), 1) // 32
    out = jnp.zeros((q, 128), i32)
    for g in range(4):
        part = value[g * q : (g + 1) * q]
        out = jnp.where(group == g, pltpu.roll(part, 32 * g, 1) if g else part, out)
    return out


def unfold(value):
    return jnp.concatenate([pltpu.roll(value, 128 - 32 * g, 1) if g else value for g in range(4)], axis=0)


def crown_rows(value, code):
    q = quantized(value, code)
    half = value.shape[1] // 2
    packed = pair(q[:, :half], q[:, half:])
    return jnp.concatenate([packed[:, n : n + 128] for n in range(0, half, 128)], axis=0)


def crown_values(rows, levels, code):
    parts = [rows[n : n + levels] for n in range(0, rows.shape[0], levels)]
    size = step_size(code)
    return jnp.concatenate([upper(p) * size for p in parts] + [lower(p) * size for p in parts], axis=1)


def peak_code(value):
    return level_code(jnp.max(jnp.max(jnp.abs(value), axis=1, keepdims=True), axis=0, keepdims=True))


def contrib_kernel(slots, band, tiles, innov, dest, cells, contrib, where_, crown):
    rays, blocks = innov.shape
    width = cells.shape[0]
    total = tiles.shape[1]
    levels = total // width
    _, band_id = spot()
    bands = contrib.shape[0] // slots
    high = bands // LOW
    square = (blocks, blocks)
    across = dest[...]
    same = iota(square, 0) == iota(square, 1)
    down = jnp.sum(jnp.where(same, across, 0), axis=1, keepdims=True)
    earlier = (across == down) & (iota(square, 0) < iota(square, 1))
    order = jnp.sum(jnp.where(earlier, 1, 0), axis=0, keepdims=True)
    apart = across ^ band_id
    slot = ((apart & (LOW - 1)) * high + apart // LOW) * slots + order
    rows = contrib.shape[0]
    pick = (iota((rows, blocks), 0) == slot).astype(f32).astype(bf16)
    long = blocks * rays
    flip = ((0,), (0,))
    both = ((1,), (1,))
    repeat = (iota((rays, long), 1) % rays == iota((rays, long), 0)).astype(f32).astype(bf16)
    spread = mm(innov[...], repeat, flip)
    spread = jnp.where(iota((blocks, long), 1) // rays == iota((blocks, long), 0), spread, 0.0).astype(bf16)
    weights = mm(pick, spread).astype(bf16)
    contrib[...] = mm(weights, tiles[...])
    place = (iota((width, 128), 0) == iota((width, 128), 1)).astype(f32).astype(bf16)
    bytes_ = [part.astype(f32).astype(bf16) for part in (cells[...] // 256, cells[...] % 256)]
    byte = [mm(mm(pick, part, both).astype(bf16), place) for part in bytes_]
    where_[...] = (byte[0] * 256.0 + byte[1]).astype(i32)

    edge = crown.shape[2]
    begin = ((band_id & (LOW - 1)) * high + band_id // LOW) * slots
    mine = (iota((slots, blocks), 0) + begin == slot).astype(f32).astype(bf16)
    near = mm(mm(mine, spread).astype(bf16), tiles[...])
    stack = jnp.concatenate([jnp.broadcast_to(near[j : j + 1], (levels, total)) for j in range(slots)], axis=0)
    tall = slots * levels
    stack = jnp.where(iota((tall, total), 1) // width == iota((tall, total), 0) % levels, stack, 0.0)
    count = slots * width
    fold = (iota((total, count), 0) % width == iota((total, count), 1) % width).astype(f32).astype(bf16)
    parts = halves(stack)
    wide = mm(parts[0], fold) + mm(parts[1], fold)
    wide = jnp.where(iota((tall, count), 1) // width == iota((tall, count), 0) // levels, wide, 0.0)
    entry = sum(wide[j * levels : (j + 1) * levels] for j in range(slots))
    tile = (iota((width, count), 0) == iota((width, count), 1) % width).astype(f32).astype(bf16)
    byte = [mm(mm(mine, part, both).astype(bf16), tile) for part in bytes_]
    spots = byte[0] * 256.0 + byte[1]
    spots = jnp.where(iota((slots, count), 1) // width == iota((slots, count), 0), spots, 0.0)
    spots = jnp.sum(spots, axis=0, keepdims=True).astype(i32)
    line, column = spots // edge, spots % edge
    chart = (iota((edge, count), 0) == column).astype(f32).astype(bf16)
    faces = crown.shape[0]
    picked = jnp.concatenate([jnp.where(line == f * band, entry, 0.0) for f in range(faces)], axis=0)
    parts = halves(picked)
    result = mm(parts[0], chart, both) + mm(parts[1], chart, both)
    for f in range(faces):
        crown[f] = result[f * levels : (f + 1) * levels]


def pack_kernel(slots, contrib, where_, crown, a, cx, cy, traded, *refs):
    sends, below, wrap, y_top, hold = refs[:LOW], *refs[LOW:]
    levels, faces, _, edge = a.shape
    first, band_id = spot()
    bands = contrib.shape[0] // slots
    high = bands // LOW
    band = edge // bands

    def row(ref, f, r):
        return ref[:, f, r, :]

    lane = iota((levels, edge), 1)
    cross = traded[:, :edge]
    side0 = traded[:, 2 * edge : 2 * edge + 1]
    corner = [row(a, f, 0)[:, 0:1] * row(cx, f, 0)[:, 0:1] for f in (1, 2)] + [side0]
    ups, ys, mids = [], [], []
    for f in range(faces):
        a0, x0, y0 = row(a, f, 0), row(cx, f, 0), row(cy, f, 0)
        up = y0 * a0
        flow = jnp.where(lane == edge - 1, corner[f], pltpu.roll(x0 * a0, edge - 1, 1))
        mids.append((1.0 - x0 - y0) * a0 + flow + row(a, f, 1) * row(cy, f, 1))
        ups.append(up)
        ys.append(y0)
        below[f] = up
        y_top[f] = y0
    far = cross[:, edge - 1 :]
    at_left = lane == 0
    left = (
        jnp.where(first, far, 0.0),
        jnp.where(first, 0.0, far),
        jnp.where(first, ups[0][:, edge - 1 :], 0.0),
    )
    again = [ys[f] * (mids[f] + jnp.where(at_left, left[f], 0.0)) for f in range(faces)]

    def of(values, one, two):
        return jnp.where(first, values[one], values[two])

    wrap[0] = of(ups, 1, 0)
    wrap[1] = jnp.where(first, traded[:, edge : 2 * edge], 0.0)
    wrap[2] = of(ys, 1, 0)
    wrap[3] = jnp.where(first, 0.0, ys[2])
    wrap[4] = of(again, 1, 0)
    wrap[5] = jnp.where(first, 0.0, again[2])
    source = band_id == 0
    local = source & first
    adds = [crown[f] for f in range(faces)]
    kinds = [adds[0], of(adds, 2, 1)]
    kinds += [
        jnp.where(ok, v, 0.0)
        for ok, v in (
            (local, ups[0]),
            (source, cross),
            (local, ys[0]),
            (source, of(ys, 2, 1)),
            (local, again[0]),
            (source, of(again, 2, 1)),
        )
    ]
    slim = iota((levels, 128), 1) // band
    wide = iota((1, 128), 1)
    code = jnp.zeros((1, 128), f32)
    codes_at = jnp.zeros((1, 128), f32)
    for n, kind in enumerate(kinds):
        this = peak_code(kind)
        code = jnp.where(slim[:1] == n, this, code)
        codes_at = jnp.where(wide == KINDS + n, this, codes_at)
    for b in range(bands):
        low_at = edge - band * (b + 1)
        half, off = low_at // 128, low_at % 128
        tile = jnp.zeros((levels, 128), f32)
        for n, kind in enumerate(kinds):
            part = kind[:, half * 128 : half * 128 + 128]
            move = (n * band - off) % 128
            tile = jnp.where(slim == n, pltpu.roll(part, move, 1) if move else part, tile)
        q = quantized(tile, code)
        hold[b] = pair(q[: levels // 2], q[levels // 2 :])
    straight = []
    for n, value in enumerate((of(adds, 1, 0), adds[2])):
        this = peak_code(value)
        codes_at = jnp.where(wide == 2 * KINDS + n, this, codes_at)
        straight.append(crown_rows(value, this))
    codes_at = codes_at.astype(i32)

    n = high * slots
    total = contrib.shape[1]
    half = total // 2
    quarter = half // 2
    for k in range(LOW):
        out = sends[k]
        block = contrib[k * n : (k + 1) * n, :]
        column = iota((n, 128), 1)
        mark = jnp.broadcast_to(codes_at, (n, 128))
        for h in range(2):
            values = block[:, h * half : (h + 1) * half]
            c = level_code(jnp.max(jnp.abs(values), axis=1, keepdims=True))
            q = quantized(values, c)
            out[h * n : (h + 1) * n, :] = pair(q[:, :quarter], q[:, quarter:])
            mark = jnp.where(column == h, c.astype(i32), mark)
        at = 2 * n
        out[at : at + n // 4, :] = fold(pair(mark, where_[k * n : (k + 1) * n, :]))
        at = at + n // 4
        for m in range(high):
            out[at + KINDS * m : at + KINDS * (m + 1), :] = hold[band_id ^ (m * LOW + k)]
        at = at + KINDS * high
        for value in straight:
            out[at : at + value.shape[0], :] = value
            at = at + value.shape[0]


def code_in(tags, lane):
    return lax.shift_right_arithmetic(tags[0:1], 16)[:, lane : lane + 1].astype(f32)


def crown_sum(levels, tags, rows):
    size = rows[0].shape[0] // 2
    return [
        sum(crown_values(r[n * size : (n + 1) * size], levels, code_in(t, 2 * KINDS + n)) for t, r in zip(tags, rows))
        for n in range(2)
    ]


def regroup_kernel(slots, high, levels, *refs):
    got, sends = refs[:LOW], refs[LOW:]
    n, w = high * slots, LOW * slots
    at = 2 * n + n // 4
    tags = [unfold(ref[2 * n : at, :]) for ref in got]
    crown_at = at + KINDS * high
    sums = crown_sum(levels, tags, [ref[crown_at:, :] for ref in got])
    codes = [peak_code(value) for value in sums]
    straight = jnp.concatenate([crown_rows(value, code) for value, code in zip(sums, codes)], axis=0)
    wide = iota((slots, 128), 1)
    for m in range(high):
        out = sends[m]
        parts = []
        for k in range(LOW):
            for h in range(2):
                out[h * w + k * slots : h * w + (k + 1) * slots, :] = got[k][h * n + m * slots : h * n + (m + 1) * slots, :]
            part = tags[k][m * slots : (m + 1) * slots]
            if k == 0:
                for c in range(2):
                    part = jnp.where(wide == 2 * KINDS + 2 + c, pair(codes[c].astype(i32), part), part)
            parts.append(part)
            to = 2 * w + w // 4 + KINDS * k
            out[to : to + KINDS, :] = got[k][at + KINDS * m : at + KINDS * (m + 1), :]
        out[2 * w : 2 * w + w // 4, :] = fold(jnp.concatenate(parts, axis=0))
        out[2 * w + w // 4 + KINDS * LOW :, :] = straight


def step_level(field, x, y, last_column, last_row):
    faces = len(field)
    band, edge = field[0].shape
    along = [x[f] * field[f] for f in range(faces)]
    upward = [y[f] * field[f] for f in range(faces)]
    shape = (band, edge)
    at_right, at_bottom = iota(shape, 1) == edge - 1, iota(shape, 0) == band - 1
    outs = []
    for f in range(faces):
        flow = pltpu.roll(along[f], edge - 1, 1)
        column = along[f + 1][:, 0:1] if f < faces - 1 else last_column
        flow = jnp.where(at_right, column, flow)
        lift = pltpu.roll(upward[f], band - 1, 0)
        lift = jnp.where(at_bottom, last_row[f], lift)
        outs.append((1.0 - x[f] - y[f]) * field[f] + flow + lift)
    return outs


def mid_kernel(a, cx, cy, below, traded, mid, mid_top, mid_side, x_side):
    levels, faces, band, edge = a.shape
    for level in range(levels):
        column = to_rows(traded[level : level + 1, 2 * edge :], 0, band, False)
        rows = [below[f, level : level + 1, :] for f in range(faces)]
        outs = step_level([a[level, f] for f in range(faces)], cx[level], cy[level], column, rows)
        for f in range(faces):
            mid[level, f] = outs[f]
            mid_top[f, level : level + 1, :] = outs[f][0:1]
        mid_side[level : level + 1, :] = to_lanes(outs[0][:, 0:1], 0, 128)
        x_side[level : level + 1, :] = to_lanes(cx[level, 0, :, 0:1], 0, 128)


def near_kernel(slots, width, high, *refs):
    got = refs[:high]
    mid_top, mid_side, x_side, y_top, wrap = refs[high : high + 5]
    below, trade, flat, spots_, charts, seams, last = refs[high + 5 :]
    faces, levels, edge = mid_top.shape
    first, _ = spot()
    w = LOW * slots
    total = high * w
    at = 2 * w + w // 4
    tags = [unfold(ref[2 * w : at, :]) for ref in got]
    tag = jnp.concatenate(tags, axis=0)
    mark = lax.shift_right_arithmetic(tag, 16)
    for h in range(2):
        packed = jnp.concatenate([ref[h * w : (h + 1) * w, :] for ref in got], axis=0)
        size = step_size(mark[:, h : h + 1].astype(f32))
        for p, value in enumerate((upper(packed), lower(packed))):
            value = jnp.transpose(value * size)
            first_part = value.astype(bf16).astype(f32)
            lines = slice((2 * h + p) * 128, (2 * h + p + 1) * 128)
            flat[0, lines, :] = first_part
            flat[1, lines, :] = value - first_part
    spots = jnp.transpose((tag & 0xFFFF).astype(f32))[:width].astype(i32)
    spots_[...] = spots
    seam = jnp.zeros((levels, 128), f32)
    group = iota((1, 128), 1) // (128 // KINDS)
    for tags_m, ref in zip(tags, got):
        for k in range(LOW):
            line = lax.shift_right_arithmetic(tags_m[k * slots : k * slots + 1], 16).astype(f32)
            code = jnp.zeros((1, 128), f32)
            for n in range(KINDS):
                code = jnp.where(group == n, line[:, KINDS + n : KINDS + n + 1], code)
            piece = ref[at + KINDS * k : at + KINDS * (k + 1), :]
            seam = seam + jnp.concatenate([upper(piece), lower(piece)], axis=0) * step_size(code)
    band = 128 // KINDS
    again = pltpu.roll(seam, 128 - 6 * band, 1) + pltpu.roll(seam, 128 - 4 * band, 1) * seam
    seams[0] = seam
    seams[1] = again
    straight = crown_sum(levels, [pltpu.roll(t, 126, 1) for t in tags], [ref[at + KINDS * LOW :, :] for ref in got])
    straight = [wrap[4 + n] + wrap[2 + n] * straight[n] for n in range(2)]
    last[...] = straight[0]
    trade[:, 128:] = straight[1]
    line, column = spots // edge, spots % edge
    for k in range(width):
        charts[:, k * total : (k + 1) * total] = (iota((edge, total), 0) == column[k : k + 1]).astype(f32).astype(bf16)
    both = ((1,), (1,))
    tops = [jnp.zeros((levels, edge), f32) for _ in range(faces)]
    side = jnp.zeros((levels, 128), f32)
    step = 4
    for k0 in range(0, width, step):
        parts, sides, lefts = [], [], []
        for k in range(k0, k0 + step):
            value = [flat[p, pl.ds(k, levels, stride=width), :] for p in range(2)]
            parts.append(jnp.concatenate([jnp.where(line[k : k + 1] == f * band, v, 0.0) for f in range(faces) for v in value], axis=0))
            sides.append(jnp.concatenate(value, axis=0))
            lefts.append((spots[k : k + 1] == iota((128, total), 0) * edge).astype(f32) * (iota((128, total), 0) < band).astype(f32))
        chart = charts[:, k0 * total : (k0 + step) * total]
        done = mm(jnp.concatenate(parts, axis=1).astype(bf16), chart, both)
        edge_done = mm(jnp.concatenate(sides, axis=1).astype(bf16), jnp.concatenate(lefts, axis=1).astype(bf16), both)
        for f in range(faces):
            tops[f] = tops[f] + done[2 * f * levels : (2 * f + 1) * levels] + done[(2 * f + 1) * levels : (2 * f + 2) * levels]
        side = side + edge_done[:levels] + edge_done[levels:]
    at_left = iota((levels, edge), 1) == 0
    turn = band - 1
    cross0, local0 = seam[:, 3 * band + turn : 3 * band + turn + 1], seam[:, 2 * band + turn : 2 * band + turn + 1]
    columns = (jnp.where(first, cross0, 0.0), jnp.where(first, 0.0, cross0), local0)
    for f in range(faces):
        value = mid_top[f] + tops[f] + jnp.where(at_left, columns[f], 0.0)
        below[f] = value * y_top[f]
    lane = iota((levels, 128), 1)
    back = (iota((128, 128), 0) + iota((128, 128), 1) == 4 * band - 1).astype(f32) * (iota((128, 128), 1) < band).astype(f32)
    parts = halves(seam)
    turned = mm(parts[0], back.astype(bf16)) + mm(parts[1], back.astype(bf16))
    value = mid_side[...] + side + jnp.where(first, turned, 0.0)
    value = value + jnp.where(lane == turn, wrap[1][:, 0:1], 0.0)
    trade[:, :128] = jnp.where(lane < band, value * x_side[...], jnp.where(lane < 2 * band, again, 0.0))


def force_kernel(flat, spots_, charts, seams, wrap, last, mid, cx, cy, result, lines, field):
    levels, faces, band, edge = mid.shape
    width, total = spots_.shape
    first, _ = spot()
    line = spots_[...] // edge
    both = ((1,), (1,))
    rest = faces * levels * band
    for f in range(faces):
        hit = [(iota((band, total), 0) + f * band == line[k : k + 1]).astype(f32) for k in range(width)]

        def fill(level, carry, f=f, hit=hit):
            at = pl.multiple_of((f * levels + level) * band, band)
            for k in range(width):
                for p in range(2):
                    value = flat[p, pl.ds(level * width + k, 1), :]
                    lines[pl.ds(at + p * rest, band), k * total : (k + 1) * total] = (hit[k] * value).astype(bf16)
            return carry

        lax.fori_loop(0, levels, fill, 0)
    field[...] = mm(lines[...], charts[...], both)
    shape_ = (band, edge)
    at_left, at_bottom = iota(shape_, 1) == 0, iota(shape_, 0) == band - 1
    zero_column = jnp.zeros((band, 1), f32)
    zero_row = jnp.zeros((1, edge), f32)
    for level in range(levels):
        one = slice(level, level + 1)
        now, later = seams[0, one, :], seams[1, one, :]
        local = to_rows(now, 2 * band, band, True)
        cross = to_rows(now, 3 * band, band, True)
        columns = (jnp.where(first, cross, 0.0), jnp.where(first, 0.0, cross), local)
        here, far = wrap[0, one, :], wrap[1, one, :]
        rows = (far, jnp.where(first, 0.0, here), jnp.where(first, here, 0.0))
        faces_now = []
        for f in range(faces):
            at = (f * levels + level) * band
            value = mid[level, f] + field[at : at + band, :] + field[at + rest : at + rest + band, :]
            value = value + jnp.where(at_left, columns[f], 0.0) + jnp.where(at_bottom, rows[f], 0.0)
            faces_now.append(value)
        here = last[one, :]
        outs = step_level(faces_now, cx[level], cy[level], zero_column, [zero_row, jnp.where(first, 0.0, here), jnp.where(first, here, 0.0)])
        outs[2] = outs[2] + jnp.where(at_left, to_rows(later, 0, band, True), 0.0)
        for f in range(faces):
            result[level, f] = outs[f]


def final_kernel(part, below, traded, out):
    levels, faces, band, edge = part.shape
    first, _ = spot()
    shape_ = (band, edge)
    at_left, at_right, at_bottom = iota(shape_, 1) == 0, iota(shape_, 1) == edge - 1, iota(shape_, 0) == band - 1
    for level in range(levels):
        one = slice(level, level + 1)
        line = traded[one, :128]
        side = to_rows(line, 0, band, False)
        cross = to_rows(line, band, band, True)
        columns = (jnp.where(first, cross, 0.0), jnp.where(first, 0.0, cross))
        for f in range(faces):
            row = below[f, one, :]
            if f == 0:
                row = row + jnp.where(first, traded[one, 128:], 0.0)
            value = part[level, f] + jnp.where(at_bottom, row, 0.0)
            if f < 2:
                value = value + jnp.where(at_left, columns[f], 0.0)
            else:
                value = value + jnp.where(at_right, side, 0.0)
            out[level, f] = value


def call(kernel, outs, args, scratch=(), specs=None, room=8, grid=(), flops=0):
    return pl.pallas_call(
        kernel,
        out_shape=outs,
        in_specs=specs or [VMEM] * len(args),
        out_specs=jax.tree.map(lambda _: VMEM, outs),
        scratch_shapes=scratch,
        grid=grid,
        cost_estimate=pl.CostEstimate(flops=flops, bytes_accessed=flops, transcendentals=0) if flops else None,
        compiler_params=pltpu.CompilerParams(vmem_limit_bytes=room << 20),
    )(*args)


def shape(dims, kind=f32):
    return jax.ShapeDtypeStruct(dims, kind)


def strip(levels, faces, rows, edge):
    return pl.BlockSpec((levels, faces, rows, edge), lambda _: (0, 0, 0, 0))


def exchange(value, apart):
    count = lax.axis_size("rows")
    return lax.ppermute(value, "rows", [(i, i ^ apart) for i in range(count)])


def shift_up(value):
    return lax.ppermute(value, "rows", [(i, i - 1) for i in range(1, lax.axis_size("rows"))])


def first_to_last(value):
    return lax.ppermute(value, "rows", [(0, lax.axis_size("rows") - 1)])


def swap_faces(value):
    return lax.ppermute(value, "face", [(0, 1), (1, 0)])


def per_device(final_adjoint, courant_x, courant_y, ray_tiles, ray_innov, ray_dest, ray_cols):
    a, cx, cy = final_adjoint, courant_x, courant_y
    levels, faces, band, edge = a.shape
    bands = lax.axis_size("rows")
    blocks, rays, total = ray_tiles.shape[1:]
    width = ray_cols.shape[2]
    slots = max(2, 2 * blocks // bands)
    high = bands // LOW
    top = strip(levels, faces, 8, edge)
    hbm = pl.BlockSpec(memory_space=pltpu.HBM)
    early = call(
        edge_kernel,
        shape((levels, 2 * edge + 128)),
        (a, cx, cy),
        specs=[hbm] * 3,
        scratch=[pltpu.VMEM((levels, faces, 8, edge), f32)] * 2
        + [pltpu.VMEM((levels, band, 128), f32)] * 2
        + [pltpu.SemaphoreType.DMA((4,))],
    )
    traded = swap_faces(early)
    count = bands * slots
    contrib, where_, crown = call(
        functools.partial(contrib_kernel, slots, band),
        (shape((count, total)), shape((count, 128), i32), shape((faces, levels, edge))),
        (ray_tiles[0].reshape(blocks * rays, total), ray_innov[0].T, ray_dest[0].T, ray_cols[0].T),
    )
    straight = 2 * levels * edge // 256
    each = high * slots
    rows = 2 * each + each // 4 + high * KINDS + straight
    edge_rows = shape((faces, levels, edge))
    *packed, below, wrap, y_top = call(
        functools.partial(pack_kernel, slots),
        (shape((rows, 128), i32),) * LOW + (edge_rows, shape((6, levels, edge)), edge_rows),
        (contrib, where_, crown, a, cx, cy, traded),
        scratch=[pltpu.VMEM((bands, KINDS, 128), i32)],
        specs=[VMEM] * 3 + [top] * 3 + [VMEM],
        grid=(1,),
    )
    got = [packed[0]] + [exchange(packed[k], k) for k in range(1, LOW)]
    each = LOW * slots
    rows = 2 * each + each // 4 + LOW * KINDS + straight
    sends = call(
        functools.partial(regroup_kernel, slots, high, levels),
        (shape((rows, 128), i32),) * high,
        got,
    )
    below_got = shift_up(below)
    wrap_got = first_to_last(wrap)
    arrived = [sends[0]] + [exchange(sends[m], m * LOW) for m in range(1, high)]
    side = shape((levels, 128))
    mid, mid_top, mid_side, x_side = call(
        mid_kernel, (shape(a.shape), edge_rows, side, side), (a, cx, cy, below_got, traded)
    )
    below, trade, *rest = call(
        functools.partial(near_kernel, slots, width, high),
        (
            edge_rows,
            shape((levels, 128 + edge)),
            shape((2, total, count)),
            shape((width, count), i32),
            shape((edge, width * count), bf16),
            shape((2, levels, 128)),
            shape((levels, edge)),
        ),
        (*arrived, mid_top, mid_side, x_side, y_top, wrap_got),
        room=16,
    )
    below_got = shift_up(below)
    trade_got = swap_faces(trade)
    flat, spots, charts, seams, last = rest
    lines = 2 * levels * faces * band
    part = call(
        force_kernel,
        shape(a.shape),
        (flat, spots, charts, seams, wrap_got, last, mid, cx, cy),
        scratch=[pltpu.VMEM((lines, width * count), bf16), pltpu.VMEM((lines, edge), f32)],
        room=32,
        flops=2 * lines * width * count * edge,
    )
    return call(final_kernel, shape(a.shape), (part, below_got, trade_got))


def solution(mesh):
    placed = (
        P(None, "face", "rows", None),
        P(None, "face", "rows", None),
        P(None, "face", "rows", None),
        P("face", "rows", None, None),
        P("face", "rows", None),
        P("face", "rows", None),
        P("face", "rows", None),
    )
    return jax.shard_map(
        per_device,
        mesh=mesh,
        in_specs=placed,
        out_specs=P(None, "face", "rows", None),
        check_vma=False,
    )
```

```python
import functools

import jax
import jax.numpy as jnp
from jax import lax
from jax.experimental import pallas as pl
from jax.experimental.pallas import tpu as pltpu
from jax.sharding import PartitionSpec as P


LOW = 4
KINDS = 8
VMEM = pl.BlockSpec(memory_space=pltpu.VMEM)
f32, bf16, i32 = jnp.float32, jnp.bfloat16, jnp.int32


def iota(shape, dim):
    return lax.broadcasted_iota(i32, shape, dim)


def spot():
    return lax.axis_index("face") == 0, lax.axis_index("rows")


def mm(x, y, dims=((1,), (0,))):
    return lax.dot_general(x, y, (dims, ((), ())), preferred_element_type=f32)


def halves(value):
    high = value.astype(bf16)
    return high, (value - high.astype(f32)).astype(bf16)


def level_code(top):
    return jnp.floor(16.0 * jnp.log2(jnp.maximum(top, 1e-30)) + 1.25)


def quantized(value, code):
    return jnp.floor(value * (32767.0 * jnp.exp2(code * (-1.0 / 16.0))) + 0.5).astype(i32)


def step_size(code):
    return jnp.exp2(code * (1.0 / 16.0)) * (1.0 / 32767.0)


def pair(first, second):
    return lax.shift_left(first, 16) | (second & 0xFFFF)


def upper(packed):
    return lax.shift_right_arithmetic(packed, 16).astype(f32)


def lower(packed):
    return lax.shift_right_arithmetic(lax.shift_left(packed, 16), 16).astype(f32)


def to_rows(line, base, band, flip):
    shape = (band, line.shape[1])
    row = iota(shape, 0)
    want = base + (band - 1 - row if flip else row)
    return jnp.sum(jnp.where(iota(shape, 1) == want, line, 0.0), axis=1, keepdims=True)


def to_lanes(column, base, width):
    shape = (column.shape[0], width)
    return jnp.sum(jnp.where(iota(shape, 1) == iota(shape, 0) + base, column, 0.0), axis=0, keepdims=True)


def edge_kernel(a, x, y, out, a_top, y_top, a_left, x_left, arrived):
    first, _ = spot()
    levels, edge = a.shape[0], a.shape[3]
    copies = [
        pltpu.make_async_copy(a.at[:, :, 0:8, :], a_top, arrived.at[0]),
        pltpu.make_async_copy(y.at[:, :, 0:8, :], y_top, arrived.at[1]),
        pltpu.make_async_copy(a.at[:, 0, :, 0:128], a_left, arrived.at[2]),
        pltpu.make_async_copy(x.at[:, 0, :, 0:128], x_left, arrived.at[3]),
    ]
    for copy in copies:
        copy.start()
    for copy in copies:
        copy.wait()
    row = [a_top[:, f, 0, :] * y_top[:, f, 0, :] for f in range(3)]
    out[:, :edge] = jnp.where(first, row[2], row[1])
    band = a.shape[2]
    for level in range(levels):
        column = (a_left[level] * x_left[level])[:, 0:1]
        line = to_lanes(column, 0, 128)
        lane = iota((1, 128), 1)
        line = jnp.where(lane == 2 * band, row[0][level : level + 1, 0:1], line)
        out[level : level + 1, edge:] = jnp.where(lane == 2 * band + 1, x_left[level][band - 1 :, 0:1], line)


def fold(value):
    q = value.shape[0] // 4
    group = iota((q, 128), 1) // 32
    out = jnp.zeros((q, 128), i32)
    for g in range(4):
        part = value[g * q : (g + 1) * q]
        out = jnp.where(group == g, pltpu.roll(part, 32 * g, 1) if g else part, out)
    return out


def unfold(value):
    return jnp.concatenate([pltpu.roll(value, 128 - 32 * g, 1) if g else value for g in range(4)], axis=0)


def peak_code(value):
    return level_code(jnp.max(jnp.max(jnp.abs(value), axis=1, keepdims=True), axis=0, keepdims=True))


def contrib_kernel(slots, band, source, innov, dest, cells, contrib, where_, crown, tiles, arrived):
    copy = pltpu.make_async_copy(source, tiles, arrived)
    copy.start()
    rays, blocks = innov.shape
    width = cells.shape[0]
    total = tiles.shape[1]
    levels = total // width
    _, band_id = spot()
    bands = contrib.shape[0] // slots
    high = bands // LOW
    square = (blocks, blocks)
    across = dest[...]
    same = iota(square, 0) == iota(square, 1)
    down = jnp.sum(jnp.where(same, across, 0), axis=1, keepdims=True)
    earlier = (across == down) & (iota(square, 0) < iota(square, 1))
    order = jnp.sum(jnp.where(earlier, 1, 0), axis=0, keepdims=True)
    apart = across ^ band_id
    slot = ((apart & (LOW - 1)) * high + apart // LOW) * slots + order
    rows = contrib.shape[0]
    pick = (iota((rows, blocks), 0) == slot).astype(f32).astype(bf16)
    long = blocks * rays
    flip = ((0,), (0,))
    both = ((1,), (1,))
    repeat = (iota((rays, long), 1) % rays == iota((rays, long), 0)).astype(f32).astype(bf16)
    spread = mm(innov[...], repeat, flip)
    spread = jnp.where(iota((blocks, long), 1) // rays == iota((blocks, long), 0), spread, 0.0).astype(bf16)
    weights = mm(pick, spread).astype(bf16)
    place = (iota((width, 128), 0) == iota((width, 128), 1)).astype(f32).astype(bf16)
    bytes_ = [part.astype(f32).astype(bf16) for part in (cells[...] // 256, cells[...] % 256)]
    byte = [mm(mm(pick, part, both).astype(bf16), place) for part in bytes_]
    where_[...] = (byte[0] * 256.0 + byte[1]).astype(i32)

    edge = crown.shape[2]
    begin = ((band_id & (LOW - 1)) * high + band_id // LOW) * slots
    mine = (iota((slots, blocks), 0) + begin == slot).astype(f32).astype(bf16)
    copy.wait()
    contrib[...] = mm(weights, tiles[...])
    near = mm(mm(mine, spread).astype(bf16), tiles[...])
    stack = jnp.concatenate([jnp.broadcast_to(near[j : j + 1], (levels, total)) for j in range(slots)], axis=0)
    tall = slots * levels
    stack = jnp.where(iota((tall, total), 1) // width == iota((tall, total), 0) % levels, stack, 0.0)
    count = slots * width
    fold = (iota((total, count), 0) % width == iota((total, count), 1) % width).astype(f32).astype(bf16)
    parts = halves(stack)
    wide = mm(parts[0], fold) + mm(parts[1], fold)
    wide = jnp.where(iota((tall, count), 1) // width == iota((tall, count), 0) // levels, wide, 0.0)
    entry = sum(wide[j * levels : (j + 1) * levels] for j in range(slots))
    tile = (iota((width, count), 0) == iota((width, count), 1) % width).astype(f32).astype(bf16)
    byte = [mm(mm(mine, part, both).astype(bf16), tile) for part in bytes_]
    spots = byte[0] * 256.0 + byte[1]
    spots = jnp.where(iota((slots, count), 1) // width == iota((slots, count), 0), spots, 0.0)
    spots = jnp.sum(spots, axis=0, keepdims=True).astype(i32)
    line, column = spots // edge, spots % edge
    chart = (iota((edge, count), 0) == column).astype(f32).astype(bf16)
    faces = crown.shape[0]
    picked = jnp.concatenate([jnp.where(line == f * band, entry, 0.0) for f in range(faces)], axis=0)
    parts = halves(picked)
    result = mm(parts[0], chart, both) + mm(parts[1], chart, both)
    for f in range(faces):
        crown[f] = result[f * levels : (f + 1) * levels]


def pack_kernel(slots, contrib, where_, crown, a, cx, cy, traded, *refs):
    sends, top, y_top, hold = refs[:LOW], *refs[LOW:]
    levels, faces, _, edge = a.shape
    first, band_id = spot()
    bands = contrib.shape[0] // slots
    high = bands // LOW
    band = edge // bands

    def row(ref, f, r):
        return ref[:, f, r, :]

    lane = iota((levels, edge), 1)
    cross = traded[:, :edge]
    side0 = traded[:, edge : edge + 1]
    corner = [row(a, f, 0)[:, 0:1] * row(cx, f, 0)[:, 0:1] for f in (1, 2)] + [side0]
    ups, ys, mids = [], [], []
    for f in range(faces):
        a0, x0, y0 = row(a, f, 0), row(cx, f, 0), row(cy, f, 0)
        up = y0 * a0
        flow = jnp.where(lane == edge - 1, corner[f], pltpu.roll(x0 * a0, edge - 1, 1))
        mids.append((1.0 - x0 - y0) * a0 + flow + row(a, f, 1) * row(cy, f, 1))
        ups.append(up)
        ys.append(y0)
        top[f] = up
        y_top[f] = y0
    far = cross[:, edge - 1 :]
    at_left = lane == 0
    left = (
        jnp.where(first, far, 0.0),
        jnp.where(first, 0.0, far),
        jnp.where(first, ups[0][:, edge - 1 :], 0.0),
    )
    again = [ys[f] * (mids[f] + jnp.where(at_left, left[f], 0.0)) for f in range(faces)]

    def of(values, one, two):
        return jnp.where(first, values[one], values[two])

    source = band_id == 0
    local = source & first
    adds = [crown[f] for f in range(faces)]
    kinds = [adds[0], of(adds, 2, 1)]
    kinds += [
        jnp.where(ok, v, 0.0)
        for ok, v in (
            (local, ups[0]),
            (source, cross),
            (local, ys[0]),
            (source, of(ys, 2, 1)),
            (local, again[0]),
            (source, of(again, 2, 1)),
        )
    ]
    slim = iota((levels, 128), 1) // band
    wide = iota((1, 128), 1)
    code = jnp.zeros((1, 128), f32)
    codes_at = jnp.zeros((1, 128), f32)
    for n, kind in enumerate(kinds):
        this = peak_code(kind)
        code = jnp.where(slim[:1] == n, this, code)
        codes_at = jnp.where(wide == KINDS + n, this, codes_at)
    for b in range(bands):
        low_at = edge - band * (b + 1)
        half, off = low_at // 128, low_at % 128
        tile = jnp.zeros((levels, 128), f32)
        for n, kind in enumerate(kinds):
            part = kind[:, half * 128 : half * 128 + 128]
            move = (n * band - off) % 128
            tile = jnp.where(slim == n, pltpu.roll(part, move, 1) if move else part, tile)
        q = quantized(tile, code)
        hold[b] = pair(q[: levels // 2], q[levels // 2 :])
    codes_at = codes_at.astype(i32)

    n = high * slots
    total = contrib.shape[1]
    half = total // 2
    quarter = half // 2
    for k in range(LOW):
        out = sends[k]
        block = contrib[k * n : (k + 1) * n, :]
        column = iota((n, 128), 1)
        mark = jnp.broadcast_to(codes_at, (n, 128))
        for h in range(2):
            values = block[:, h * half : (h + 1) * half]
            c = level_code(jnp.max(jnp.abs(values), axis=1, keepdims=True))
            q = quantized(values, c)
            out[h * n : (h + 1) * n, :] = pair(q[:, :quarter], q[:, quarter:])
            mark = jnp.where(column == h, c.astype(i32), mark)
        at = 2 * n
        out[at : at + n // 4, :] = fold(pair(mark, where_[k * n : (k + 1) * n, :]))
        at = at + n // 4
        for m in range(high):
            out[at + KINDS * m : at + KINDS * (m + 1), :] = hold[band_id ^ (m * LOW + k)]


def seam_code(tags):
    line = lax.shift_right_arithmetic(tags[0:1], 16).astype(f32)
    group = iota((1, 128), 1) // (128 // KINDS)
    code = jnp.zeros((1, 128), f32)
    for n in range(KINDS):
        code = jnp.where(group == n, line[:, KINDS + n : KINDS + n + 1], code)
    return code


def seam_value(rows, size):
    return jnp.concatenate([upper(rows), lower(rows)], axis=0) * size


def regroup_kernel(slots, high, levels, *refs):
    got, sends = refs[:LOW], refs[LOW:]
    n, w = high * slots, LOW * slots
    at = 2 * n + n // 4
    tags = [unfold(ref[2 * n : at, :]) for ref in got]
    sizes = [step_size(seam_code(t)) for t in tags]
    wide = iota((1, 128), 1)
    group = wide // (128 // KINDS)
    to = 2 * w + w // 4
    for m in range(high):
        out = sends[m]
        tile = sum(seam_value(got[k][at + KINDS * m : at + KINDS * (m + 1), :], sizes[k]) for k in range(LOW))
        peak = jnp.max(jnp.abs(tile), axis=0, keepdims=True)
        code = mark = jnp.zeros((1, 128), f32)
        for c in range(KINDS):
            this = level_code(jnp.max(jnp.where(group == c, peak, 0.0), axis=1, keepdims=True))
            code = jnp.where(group == c, this, code)
            mark = jnp.where(wide == KINDS + c, this, mark)
        q = quantized(tile, code)
        out[to : to + KINDS, :] = pair(q[: levels // 2], q[levels // 2 :])
        mark = lax.shift_left(mark.astype(i32), 16)
        parts = []
        for k in range(LOW):
            for h in range(2):
                out[h * w + k * slots : h * w + (k + 1) * slots, :] = got[k][h * n + m * slots : h * n + (m + 1) * slots, :]
            part = tags[k][m * slots : (m + 1) * slots]
            parts.append(jnp.where(wide < KINDS, part, mark | (part & 0xFFFF)))
        out[2 * w : to, :] = fold(jnp.concatenate(parts, axis=0))


def step_level(field, x, y, last_column, last_row):
    faces = len(field)
    band, edge = field[0].shape
    along = [x[f] * field[f] for f in range(faces)]
    upward = [y[f] * field[f] for f in range(faces)]
    shape = (band, edge)
    at_right, at_bottom = iota(shape, 1) == edge - 1, iota(shape, 0) == band - 1
    outs = []
    for f in range(faces):
        flow = pltpu.roll(along[f], edge - 1, 1)
        column = along[f + 1][:, 0:1] if f < faces - 1 else last_column
        flow = jnp.where(at_right, column, flow)
        lift = pltpu.roll(upward[f], band - 1, 0)
        lift = jnp.where(at_bottom, last_row[f], lift)
        outs.append((1.0 - x[f] - y[f]) * field[f] + flow + lift)
    return outs


def mid_kernel(a, cx, cy, traded, mid, mid_top, mid_side, x_side, foot):
    levels, faces, band, edge = a.shape
    rows = [jnp.zeros((1, edge), f32)] * faces
    for level in range(levels):
        one = slice(level, level + 1)
        column = to_rows(traded[one, edge:], 0, band, False)
        outs = step_level([a[level, f] for f in range(faces)], cx[level], cy[level], column, rows)
        for f in range(faces):
            mid[level, f] = outs[f]
            mid_top[f, one, :] = outs[f][0:1]
            foot[f, one, :] = cx[level, f, band - 1 :, :]
            foot[faces + f, one, :] = cy[level, f, band - 1 :, :]
        mid_side[one, :] = to_lanes(outs[0][:, 0:1], 0, 128)
        x_side[one, :] = to_lanes(cx[level, 0, :, 0:1], 0, 128)


def near_kernel(slots, width, high, *refs):
    got = refs[:high]
    mid_top, mid_side, x_side, y_top, top, traded = refs[high : high + 6]
    below, jump, trade, flat, spots_, charts, seams = refs[high + 6 :]
    faces, levels, edge = mid_top.shape
    first, _ = spot()
    w = LOW * slots
    total = high * w
    at = 2 * w + w // 4
    tags = [unfold(ref[2 * w : at, :]) for ref in got]
    tag = jnp.concatenate(tags, axis=0)
    mark = lax.shift_right_arithmetic(tag, 16)
    for h in range(2):
        packed = jnp.concatenate([ref[h * w : (h + 1) * w, :] for ref in got], axis=0)
        size = step_size(mark[:, h : h + 1].astype(f32))
        for p, value in enumerate((upper(packed), lower(packed))):
            value = jnp.transpose(value * size)
            first_part = value.astype(bf16).astype(f32)
            lines = slice((2 * h + p) * 128, (2 * h + p + 1) * 128)
            flat[0, lines, :] = first_part
            flat[1, lines, :] = value - first_part
    spots = jnp.transpose((tag & 0xFFFF).astype(f32))[:width].astype(i32)
    spots_[...] = spots
    seam = jnp.zeros((levels, 128), f32)
    for tags_m, ref in zip(tags, got):
        seam = seam + seam_value(ref[at : at + KINDS, :], step_size(seam_code(tags_m)))
    band = 128 // KINDS
    again = pltpu.roll(seam, 128 - 6 * band, 1) + pltpu.roll(seam, 128 - 4 * band, 1) * seam
    seams[0] = seam
    seams[1] = again
    line, column = spots // edge, spots % edge
    for k in range(width):
        charts[:, k * total : (k + 1) * total] = (iota((edge, total), 0) == column[k : k + 1]).astype(f32).astype(bf16)
    both = ((1,), (1,))
    tops = [jnp.zeros((levels, edge), f32) for _ in range(faces)]
    side = jnp.zeros((levels, 128), f32)
    step = 4
    for k0 in range(0, width, step):
        parts, sides, lefts = [], [], []
        for k in range(k0, k0 + step):
            value = [flat[p, pl.ds(k, levels, stride=width), :] for p in range(2)]
            parts.append(jnp.concatenate([jnp.where(line[k : k + 1] == f * band, v, 0.0) for f in range(faces) for v in value], axis=0))
            sides.append(jnp.concatenate(value, axis=0))
            lefts.append((spots[k : k + 1] == iota((128, total), 0) * edge).astype(f32) * (iota((128, total), 0) < band).astype(f32))
        chart = charts[:, k0 * total : (k0 + step) * total]
        done = mm(jnp.concatenate(parts, axis=1).astype(bf16), chart, both)
        edge_done = mm(jnp.concatenate(sides, axis=1).astype(bf16), jnp.concatenate(lefts, axis=1).astype(bf16), both)
        for f in range(faces):
            tops[f] = tops[f] + done[2 * f * levels : (2 * f + 1) * levels] + done[(2 * f + 1) * levels : (2 * f + 2) * levels]
        side = side + edge_done[:levels] + edge_done[levels:]
    at_left = iota((levels, edge), 1) == 0
    turn = band - 1
    cross0, local0 = seam[:, 3 * band + turn : 3 * band + turn + 1], seam[:, 2 * band + turn : 2 * band + turn + 1]
    columns = (jnp.where(first, cross0, 0.0), jnp.where(first, 0.0, cross0), local0)
    for f in range(faces):
        value = mid_top[f] + tops[f] + jnp.where(at_left, columns[f], 0.0)
        below[:, f * edge : (f + 1) * edge] = top[f]
        below[:, (faces + f) * edge : (faces + f + 1) * edge] = value * y_top[f]
    below[:, 2 * faces * edge :] = pltpu.roll(traded[:, edge:], 128 - 2 * band, 1)
    jump[:, :edge] = top[faces - 1]
    jump[:, edge:] = value * y_top[faces - 1]
    lane = iota((levels, 128), 1)
    back = (iota((128, 128), 0) + iota((128, 128), 1) == 4 * band - 1).astype(f32) * (iota((128, 128), 1) < band).astype(f32)
    parts = halves(seam)
    turned = mm(parts[0], back.astype(bf16)) + mm(parts[1], back.astype(bf16))
    value = mid_side[...] + side + jnp.where(first, turned, 0.0)
    trade[...] = jnp.where(lane < band, value * x_side[...], jnp.where(lane < 2 * band, again, 0.0))


def force_kernel(flat, spots_, charts, seams, mid, cx, cy, result, lines):
    levels, faces, band, edge = mid.shape
    width, total = spots_.shape
    first, _ = spot()
    line = spots_[...] // edge
    both = ((1,), (1,))
    shape_ = (band, edge)
    at_left = iota(shape_, 1) == 0
    zero_column = jnp.zeros((band, 1), f32)
    zero_row = jnp.zeros((1, edge), f32)
    group = lines.shape[1] // (2 * faces * band)
    rest = faces * group * band

    def fill(g):
        for k in range(width):
            hit = [(iota((band, total), 0) + f * band == line[k : k + 1]).astype(f32).astype(bf16) for f in range(faces)]
            for i in range(group):
                row = (g * group + i) * width + k
                for p in range(2):
                    value = jnp.broadcast_to(flat[p, row : row + 1, :], (band, total)).astype(bf16)
                    for f in range(faces):
                        at = p * rest + (f * group + i) * band
                        lines[g % 2, at : at + band, k * total : (k + 1) * total] = hit[f] * value

    def finish(g, field):
        for i in range(group):
            level = g * group + i
            one = slice(level, level + 1)
            now, later = seams[0, one, :], seams[1, one, :]
            local = to_rows(now, 2 * band, band, True)
            cross = to_rows(now, 3 * band, band, True)
            columns = (jnp.where(first, cross, 0.0), jnp.where(first, 0.0, cross), local)
            faces_now = []
            for f in range(faces):
                at = (f * group + i) * band
                value = mid[level, f] + field[at : at + band] + field[at + rest : at + rest + band]
                value = value + jnp.where(at_left, columns[f], 0.0)
                faces_now.append(value)
            outs = step_level(faces_now, cx[level], cy[level], zero_column, [zero_row] * faces)
            outs[2] = outs[2] + jnp.where(at_left, to_rows(later, 0, band, True), 0.0)
            for f in range(faces):
                result[level, f] = outs[f]

    fill(0)
    for g in range(levels // group):
        field = mm(lines[g % 2], charts[...], both)
        if (g + 1) * group < levels:
            fill(g + 1)
        finish(g, field)


def final_kernel(part, below, jump, trade, traded, foot, out, hold, sent):
    levels, faces, band, edge = part.shape
    first, band_id = spot()
    last = band_id == lax.axis_size("rows") - 1
    shape_ = (band, edge)
    at_left, at_right = iota(shape_, 1) == 0, iota(shape_, 1) == edge - 1
    at_bottom, at_above = iota(shape_, 0) == band - 1, iota(shape_, 0) == band - 2

    def bottom(step):
        got = [below[:, (step * faces + f) * edge : (step * faces + f + 1) * edge] for f in range(faces)]
        far = jump[:, step * edge : (step + 1) * edge]
        seam = (jnp.where(first, far, 0.0), jnp.where(first, 0.0, got[0]), jnp.where(first, got[1], 0.0))
        return got, [jnp.where(last, s, g) for s, g in zip(seam, got)]

    got, one_back = bottom(0)
    _, now = bottom(1)
    partner = jnp.where(last, jnp.where(first, 0.0, got[2][:, 0:1]), below[:, 2 * faces * edge : 2 * faces * edge + 1])
    partner = partner * traded[:, edge + 2 * band + 1 : edge + 2 * band + 2]
    along = [foot[f] * one_back[f] for f in range(faces)]
    upward = [foot[faces + f] * one_back[f] for f in range(faces)]
    column = [along[1][:, 0:1], along[2][:, 0:1], partner]
    ends = iota((levels, edge), 1) == edge - 1
    for f in range(faces):
        flow = jnp.where(ends, column[f], pltpu.roll(along[f], edge - 1, 1))
        now[f] = now[f] + one_back[f] - along[f] - upward[f] + flow
    copies = []
    for level in range(levels):
        one = slice(level, level + 1)
        side = to_rows(trade[one, :], 0, band, False)
        cross = to_rows(trade[one, :], band, band, True)
        columns = (jnp.where(first, cross, 0.0), jnp.where(first, 0.0, cross))
        for f in range(faces):
            value = part[level, f] + jnp.where(at_bottom, now[f][one], jnp.where(at_above, upward[f][one], 0.0))
            if f < 2:
                value = value + jnp.where(at_left, columns[f], 0.0)
            else:
                value = value + jnp.where(at_right, side, 0.0)
            hold[level, f] = value
        if level % 4 == 3:
            block = pl.ds(level - 3, 4)
            copy = pltpu.make_async_copy(hold.at[block], out.at[block], sent.at[level // 4])
            copy.start()
            copies.append(copy)
    for copy in copies:
        copy.wait()


def call(kernel, outs, args, scratch=(), specs=None, room=8, grid=(), flops=0, out_specs=None):
    return pl.pallas_call(
        kernel,
        out_shape=outs,
        in_specs=specs or [VMEM] * len(args),
        out_specs=out_specs or jax.tree.map(lambda _: VMEM, outs),
        scratch_shapes=scratch,
        grid=grid,
        cost_estimate=pl.CostEstimate(flops=flops, bytes_accessed=flops, transcendentals=0) if flops else None,
        compiler_params=pltpu.CompilerParams(vmem_limit_bytes=room << 20),
    )(*args)


def shape(dims, kind=f32):
    return jax.ShapeDtypeStruct(dims, kind)


def strip(levels, faces, rows, edge):
    return pl.BlockSpec((levels, faces, rows, edge), lambda _: (0, 0, 0, 0))


def exchange(value, apart):
    count = lax.axis_size("rows")
    return lax.ppermute(value, "rows", [(i, i ^ apart) for i in range(count)])


def shift_up(value):
    count = lax.axis_size("rows")
    return lax.ppermute(value, "rows", [(i, (i + count - 1) % count) for i in range(count)])


def seam_jump(value):
    count = lax.axis_size("rows")
    return lax.ppermute(value, ("face", "rows"), [(count, count - 1)])


def swap_faces(value):
    return lax.ppermute(value, "face", [(0, 1), (1, 0)])


def per_device(final_adjoint, courant_x, courant_y, ray_tiles, ray_innov, ray_dest, ray_cols):
    a, cx, cy = final_adjoint, courant_x, courant_y
    levels, faces, band, edge = a.shape
    bands = lax.axis_size("rows")
    blocks, rays, total = ray_tiles.shape[1:]
    width = ray_cols.shape[2]
    slots = max(2, 2 * blocks // bands)
    high = bands // LOW
    top = strip(levels, faces, 8, edge)
    hbm = pl.BlockSpec(memory_space=pltpu.HBM)
    early = call(
        edge_kernel,
        shape((levels, edge + 128)),
        tuple(pltpu.with_memory_space_constraint(v, pltpu.HBM) for v in (a, cx, cy)),
        specs=[hbm] * 3,
        scratch=[pltpu.VMEM((levels, faces, 8, edge), f32)] * 2
        + [pltpu.VMEM((levels, band, 128), f32)] * 2
        + [pltpu.SemaphoreType.DMA((4,))],
    )
    traded = swap_faces(early)
    count = bands * slots
    contrib, where_, crown = call(
        functools.partial(contrib_kernel, slots, band),
        (shape((count, total)), shape((count, 128), i32), shape((faces, levels, edge))),
        (
            pltpu.with_memory_space_constraint(ray_tiles[0].reshape(blocks * rays, total), pltpu.HBM),
            ray_innov[0].T,
            ray_dest[0].T,
            ray_cols[0].T,
        ),
        specs=[hbm] + [VMEM] * 3,
        scratch=[pltpu.VMEM((blocks * rays, total), bf16), pltpu.SemaphoreType.DMA],
    )
    each = high * slots
    rows = 2 * each + each // 4 + high * KINDS
    edge_rows = shape((faces, levels, edge))
    *packed, first_rows, y_top = call(
        functools.partial(pack_kernel, slots),
        (shape((rows, 128), i32),) * LOW + (edge_rows, edge_rows),
        (contrib, where_, crown, a, cx, cy, traded),
        scratch=[pltpu.VMEM((bands, KINDS, 128), i32)],
        specs=[VMEM] * 3 + [top] * 3 + [VMEM],
        grid=(1,),
    )
    got = [packed[0]] + [exchange(packed[k], k) for k in range(1, LOW)]
    each = LOW * slots
    rows = 2 * each + each // 4 + KINDS
    sends = call(
        functools.partial(regroup_kernel, slots, high, levels),
        (shape((rows, 128), i32),) * high,
        got,
    )
    arrived = [sends[0]] + [exchange(sends[m], m * LOW) for m in range(1, high)]
    side = shape((levels, 128))
    mid, mid_top, mid_side, x_side, foot = call(
        mid_kernel,
        (shape(a.shape), edge_rows, side, side, shape((2 * faces, levels, edge))),
        (a, cx, cy, traded),
    )
    below, jump, trade, flat, spots, charts, seams = call(
        functools.partial(near_kernel, slots, width, high),
        (
            shape((levels, 2 * faces * edge + 128)),
            shape((levels, 2 * edge)),
            side,
            shape((2, total, count)),
            shape((width, count), i32),
            shape((edge, width * count), bf16),
            shape((2, levels, 128)),
        ),
        (*arrived, mid_top, mid_side, x_side, y_top, first_rows, traded),
        room=16,
    )
    below_got = shift_up(below)
    jump_got = seam_jump(jump)
    trade_got = swap_faces(trade)
    lines = 2 * levels * faces * band
    part = call(
        force_kernel,
        shape(a.shape),
        (flat, spots, charts, seams, mid, cx, cy),
        scratch=[pltpu.VMEM((2, lines // 4, width * count), bf16)],
        room=32,
        flops=2 * lines * width * count * edge,
    )
    return call(
        final_kernel,
        shape(a.shape),
        (part, below_got, jump_got, trade_got, traded, foot),
        scratch=[pltpu.VMEM(a.shape, f32), pltpu.SemaphoreType.DMA((levels // 4,))],
        out_specs=hbm,
    )


def solution(mesh):
    placed = (
        P(None, "face", "rows", None),
        P(None, "face", "rows", None),
        P(None, "face", "rows", None),
        P("face", "rows", None, None),
        P("face", "rows", None),
        P("face", "rows", None),
        P("face", "rows", None),
    )
    return jax.shard_map(
        per_device,
        mesh=mesh,
        in_specs=placed,
        out_specs=P(None, "face", "rows", None),
        check_vma=False,
    )
```

```python
import functools

import jax
import jax.numpy as jnp
from jax import lax
from jax.experimental import pallas as pl
from jax.experimental.pallas import tpu as pltpu
from jax.sharding import PartitionSpec as P


LOW = 4
KINDS = 8
VMEM = pl.BlockSpec(memory_space=pltpu.VMEM)
f32, bf16, i32 = jnp.float32, jnp.bfloat16, jnp.int32


def iota(shape, dim):
    return lax.broadcasted_iota(i32, shape, dim)


def spot():
    return lax.axis_index("face") == 0, lax.axis_index("rows")


def mm(x, y, dims=((1,), (0,))):
    return lax.dot_general(x, y, (dims, ((), ())), preferred_element_type=f32)


def halves(value):
    high = value.astype(bf16)
    return high, (value - high.astype(f32)).astype(bf16)


def level_code(top):
    return jnp.floor(16.0 * jnp.log2(jnp.maximum(top, 1e-30)) + 1.25)


def quantized(value, code):
    return jnp.floor(value * (32767.0 * jnp.exp2(code * (-1.0 / 16.0))) + 0.5).astype(i32)


def step_size(code):
    return jnp.exp2(code * (1.0 / 16.0)) * (1.0 / 32767.0)


def pair(first, second):
    return lax.shift_left(first, 16) | (second & 0xFFFF)


def upper(packed):
    return lax.shift_right_arithmetic(packed, 16).astype(f32)


def lower(packed):
    return lax.shift_right_arithmetic(lax.shift_left(packed, 16), 16).astype(f32)


def to_rows(line, base, band, flip):
    shape = (band, line.shape[1])
    row = iota(shape, 0)
    want = base + (band - 1 - row if flip else row)
    return jnp.sum(jnp.where(iota(shape, 1) == want, line, 0.0), axis=1, keepdims=True)


def to_lanes(column, base, width):
    shape = (column.shape[0], width)
    return jnp.sum(jnp.where(iota(shape, 1) == iota(shape, 0) + base, column, 0.0), axis=0, keepdims=True)


def edge_kernel(a, x, y, *refs):
    sources, out, heads, near, left, arrived = refs[:4], refs[4], refs[5:8], refs[8:12], refs[12:15], refs[15]
    first, band_id = spot()
    levels, edge = a.shape[0], a.shape[3]
    band = a.shape[2]
    copies = [
        pltpu.make_async_copy(a.at[:, 0, :, 0:128], left[0], arrived.at[0]),
        pltpu.make_async_copy(x.at[:, 0, :, 0:128], left[1], arrived.at[1]),
        pltpu.make_async_copy(y.at[:, 0, 0:8, 0:128], left[2], arrived.at[2]),
    ]
    top = [pltpu.make_async_copy(far.at[:, :, 0:8, :], head, arrived.at[3 + n]) for n, (far, head) in enumerate(zip((a, x, y), heads))]
    later = [pltpu.make_async_copy(far, here, arrived.at[6 + n]) for n, (far, here) in enumerate(zip(sources, near))]
    for copy in copies:
        copy.start()

    @pl.when(band_id == 0)
    def _():
        for copy in top:
            copy.start()

    for copy in later:
        copy.start()

    @pl.when(band_id != 0)
    def _():
        for head in heads:
            head[...] = jnp.zeros_like(head)
        out[:, :edge] = jnp.zeros((levels, edge), f32)

    for copy in copies:
        copy.wait()
    lane = iota((1, 128), 1)
    for level in range(levels):
        a_here, x_here = left[0][level], left[1][level]
        line = to_lanes((a_here * x_here)[:, 0:1], 0, 128)
        line = jnp.where(lane == 2 * band, a_here[0:1, 0:1] * left[2][level, 0:1, 0:1], line)
        out[level : level + 1, edge:] = jnp.where(lane == 2 * band + 1, x_here[band - 1 :, 0:1], line)

    @pl.when(band_id == 0)
    def _():
        for copy in top:
            copy.wait()
        row = [heads[0][:, f, 0, :] * heads[2][:, f, 0, :] for f in (1, 2)]
        out[:, :edge] = jnp.where(first, row[1], row[0])

    for copy in later:
        copy.wait()


def fold(value):
    q = value.shape[0] // 4
    group = iota((q, 128), 1) // 32
    out = jnp.zeros((q, 128), i32)
    for g in range(4):
        part = value[g * q : (g + 1) * q]
        out = jnp.where(group == g, pltpu.roll(part, 32 * g, 1) if g else part, out)
    return out


def unfold(value):
    return jnp.concatenate([pltpu.roll(value, 128 - 32 * g, 1) if g else value for g in range(4)], axis=0)


def peak_code(value):
    return level_code(jnp.max(jnp.max(jnp.abs(value), axis=1, keepdims=True), axis=0, keepdims=True))


def contrib_kernel(slots, band, tiles, innov, dest, cells, contrib, where_, crown):
    rays, blocks = innov.shape
    width = cells.shape[0]
    total = tiles.shape[1]
    levels = total // width
    _, band_id = spot()
    bands = contrib.shape[0] // slots
    high = bands // LOW
    square = (blocks, blocks)
    across = dest[...]
    same = iota(square, 0) == iota(square, 1)
    down = jnp.sum(jnp.where(same, across, 0), axis=1, keepdims=True)
    earlier = (across == down) & (iota(square, 0) < iota(square, 1))
    order = jnp.sum(jnp.where(earlier, 1, 0), axis=0, keepdims=True)
    apart = across ^ band_id
    slot = ((apart & (LOW - 1)) * high + apart // LOW) * slots + order
    rows = contrib.shape[0]
    pick = (iota((rows, blocks), 0) == slot).astype(f32).astype(bf16)
    long = blocks * rays
    flip = ((0,), (0,))
    both = ((1,), (1,))
    repeat = (iota((rays, long), 1) % rays == iota((rays, long), 0)).astype(f32).astype(bf16)
    spread = mm(innov[...], repeat, flip)
    spread = jnp.where(iota((blocks, long), 1) // rays == iota((blocks, long), 0), spread, 0.0).astype(bf16)
    weights = mm(pick, spread).astype(bf16)
    place = (iota((width, 128), 0) == iota((width, 128), 1)).astype(f32).astype(bf16)
    bytes_ = [part.astype(f32).astype(bf16) for part in (cells[...] // 256, cells[...] % 256)]
    byte = [mm(mm(pick, part, both).astype(bf16), place) for part in bytes_]
    where_[...] = (byte[0] * 256.0 + byte[1]).astype(i32)

    edge = crown.shape[2]
    begin = ((band_id & (LOW - 1)) * high + band_id // LOW) * slots
    mine = (iota((slots, blocks), 0) + begin == slot).astype(f32).astype(bf16)
    contrib[...] = mm(weights, tiles[...])
    near = mm(mm(mine, spread).astype(bf16), tiles[...])
    stack = jnp.concatenate([jnp.broadcast_to(near[j : j + 1], (levels, total)) for j in range(slots)], axis=0)
    tall = slots * levels
    stack = jnp.where(iota((tall, total), 1) // width == iota((tall, total), 0) % levels, stack, 0.0)
    count = slots * width
    fold = (iota((total, count), 0) % width == iota((total, count), 1) % width).astype(f32).astype(bf16)
    parts = halves(stack)
    wide = mm(parts[0], fold) + mm(parts[1], fold)
    wide = jnp.where(iota((tall, count), 1) // width == iota((tall, count), 0) // levels, wide, 0.0)
    entry = sum(wide[j * levels : (j + 1) * levels] for j in range(slots))
    tile = (iota((width, count), 0) == iota((width, count), 1) % width).astype(f32).astype(bf16)
    byte = [mm(mm(mine, part, both).astype(bf16), tile) for part in bytes_]
    spots = byte[0] * 256.0 + byte[1]
    spots = jnp.where(iota((slots, count), 1) // width == iota((slots, count), 0), spots, 0.0)
    spots = jnp.sum(spots, axis=0, keepdims=True).astype(i32)
    line, column = spots // edge, spots % edge
    chart = (iota((edge, count), 0) == column).astype(f32).astype(bf16)
    faces = crown.shape[0]
    picked = jnp.concatenate([jnp.where(line == f * band, entry, 0.0) for f in range(faces)], axis=0)
    parts = halves(picked)
    result = mm(parts[0], chart, both) + mm(parts[1], chart, both)
    for f in range(faces):
        crown[f] = result[f * levels : (f + 1) * levels]


def pack_kernel(slots, contrib, where_, crown, a, cx, cy, traded, *refs):
    sends, hold = refs[:LOW], refs[LOW]
    levels, faces, _, edge = a.shape
    first, band_id = spot()
    bands = contrib.shape[0] // slots
    high = bands // LOW
    band = edge // bands

    def row(ref, f, r):
        return ref[:, f, r, :]

    lane = iota((levels, edge), 1)
    cross = traded[:, :edge]
    side0 = traded[:, edge : edge + 1]
    corner = [row(a, f, 0)[:, 0:1] * row(cx, f, 0)[:, 0:1] for f in (1, 2)] + [side0]
    ups, ys, mids = [], [], []
    for f in range(faces):
        a0, x0, y0 = row(a, f, 0), row(cx, f, 0), row(cy, f, 0)
        up = y0 * a0
        flow = jnp.where(lane == edge - 1, corner[f], pltpu.roll(x0 * a0, edge - 1, 1))
        mids.append((1.0 - x0 - y0) * a0 + flow + row(a, f, 1) * row(cy, f, 1))
        ups.append(up)
        ys.append(y0)
    far = cross[:, edge - 1 :]
    at_left = lane == 0
    left = (
        jnp.where(first, far, 0.0),
        jnp.where(first, 0.0, far),
        jnp.where(first, ups[0][:, edge - 1 :], 0.0),
    )
    again = [ys[f] * (mids[f] + jnp.where(at_left, left[f], 0.0)) for f in range(faces)]

    def of(values, one, two):
        return jnp.where(first, values[one], values[two])

    source = band_id == 0
    local = source & first
    adds = [crown[f] for f in range(faces)]
    kinds = [adds[0], of(adds, 2, 1)]
    kinds += [
        jnp.where(ok, v, 0.0)
        for ok, v in (
            (local, ups[0]),
            (source, cross),
            (local, ys[0]),
            (source, of(ys, 2, 1)),
            (local, again[0]),
            (source, of(again, 2, 1)),
        )
    ]
    slim = iota((levels, 128), 1) // band
    wide = iota((1, 128), 1)
    code = jnp.zeros((1, 128), f32)
    codes_at = jnp.zeros((1, 128), f32)
    for n, kind in enumerate(kinds):
        this = peak_code(kind)
        code = jnp.where(slim[:1] == n, this, code)
        codes_at = jnp.where(wide == KINDS + n, this, codes_at)
    for b in range(bands):
        low_at = edge - band * (b + 1)
        half, off = low_at // 128, low_at % 128
        tile = jnp.zeros((levels, 128), f32)
        for n, kind in enumerate(kinds):
            part = kind[:, half * 128 : half * 128 + 128]
            move = (n * band - off) % 128
            tile = jnp.where(slim == n, pltpu.roll(part, move, 1) if move else part, tile)
        q = quantized(tile, code)
        hold[b] = pair(q[: levels // 2], q[levels // 2 :])
    codes_at = codes_at.astype(i32)

    n = high * slots
    total = contrib.shape[1]
    half = total // 2
    quarter = half // 2
    for k in range(LOW):
        out = sends[k]
        block = contrib[k * n : (k + 1) * n, :]
        column = iota((n, 128), 1)
        mark = jnp.broadcast_to(codes_at, (n, 128))
        for h in range(2):
            values = block[:, h * half : (h + 1) * half]
            c = level_code(jnp.max(jnp.abs(values), axis=1, keepdims=True))
            q = quantized(values, c)
            out[h * n : (h + 1) * n, :] = pair(q[:, :quarter], q[:, quarter:])
            mark = jnp.where(column == h, c.astype(i32), mark)
        at = 2 * n
        out[at : at + n // 4, :] = fold(pair(mark, where_[k * n : (k + 1) * n, :]))
        at = at + n // 4
        for m in range(high):
            out[at + KINDS * m : at + KINDS * (m + 1), :] = hold[band_id ^ (m * LOW + k)]


def seam_code(tags):
    line = lax.shift_right_arithmetic(tags[0:1], 16).astype(f32)
    group = iota((1, 128), 1) // (128 // KINDS)
    code = jnp.zeros((1, 128), f32)
    for n in range(KINDS):
        code = jnp.where(group == n, line[:, KINDS + n : KINDS + n + 1], code)
    return code


def seam_value(rows, size):
    return jnp.concatenate([upper(rows), lower(rows)], axis=0) * size


def regroup_kernel(slots, high, levels, *refs):
    got, sends = refs[:LOW], refs[LOW + 1 :]
    n, w = high * slots, LOW * slots
    at = 2 * n + n // 4
    tags = [unfold(ref[2 * n : at, :]) for ref in got]
    sizes = [step_size(seam_code(t)) for t in tags]
    wide = iota((1, 128), 1)
    group = wide // (128 // KINDS)
    to = 2 * w + w // 4
    for m in range(high):
        out = sends[m]
        tile = sum(seam_value(got[k][at + KINDS * m : at + KINDS * (m + 1), :], sizes[k]) for k in range(LOW))
        peak = jnp.max(jnp.abs(tile), axis=0, keepdims=True)
        code = mark = jnp.zeros((1, 128), f32)
        for c in range(KINDS):
            this = level_code(jnp.max(jnp.where(group == c, peak, 0.0), axis=1, keepdims=True))
            code = jnp.where(group == c, this, code)
            mark = jnp.where(wide == KINDS + c, this, mark)
        q = quantized(tile, code)
        out[to : to + KINDS, :] = pair(q[: levels // 2], q[levels // 2 :])
        mark = lax.shift_left(mark.astype(i32), 16)
        parts = []
        for k in range(LOW):
            for h in range(2):
                out[h * w + k * slots : h * w + (k + 1) * slots, :] = got[k][h * n + m * slots : h * n + (m + 1) * slots, :]
            part = tags[k][m * slots : (m + 1) * slots]
            parts.append(jnp.where(wide < KINDS, part, mark | (part & 0xFFFF)))
        out[2 * w : to, :] = fold(jnp.concatenate(parts, axis=0))


def step_level(field, x, y, last_column, last_row):
    faces = len(field)
    band, edge = field[0].shape
    along = [x[f] * field[f] for f in range(faces)]
    upward = [y[f] * field[f] for f in range(faces)]
    shape = (band, edge)
    at_right, at_bottom = iota(shape, 1) == edge - 1, iota(shape, 0) == band - 1
    outs = []
    for f in range(faces):
        flow = pltpu.roll(along[f], edge - 1, 1)
        column = along[f + 1][:, 0:1] if f < faces - 1 else last_column
        flow = jnp.where(at_right, column, flow)
        lift = pltpu.roll(upward[f], band - 1, 0)
        lift = jnp.where(at_bottom, last_row[f], lift)
        outs.append((1.0 - x[f] - y[f]) * field[f] + flow + lift)
    return outs


def mid_kernel(a_far, x_far, y_far, traded, mid, mid_top, mid_side, x_side, foot, top, y_top, cx, cy, a, arrived):
    levels, faces, band, edge = a.shape
    group = 4
    copies = []
    for g in range(levels // group):
        part = pl.ds(g * group, group)
        copies.append([pltpu.make_async_copy(far.at[part], near.at[part], arrived.at[3 * g + n]) for n, (far, near) in enumerate(((a_far, a), (x_far, cx), (y_far, cy)))])
        for copy in copies[-1]:
            copy.start()
    rows = [jnp.zeros((1, edge), f32)] * faces
    for level in range(levels):
        if level % group == 0:
            for copy in copies[level // group]:
                copy.wait()
        one = slice(level, level + 1)
        column = to_rows(traded[one, edge:], 0, band, False)
        outs = step_level([a[level, f] for f in range(faces)], cx[level], cy[level], column, rows)
        for f in range(faces):
            mid[level, f] = outs[f]
            mid_top[f, one, :] = outs[f][0:1]
            top[f, one, :] = a[level, f, 0:1, :] * cy[level, f, 0:1, :]
            y_top[f, one, :] = cy[level, f, 0:1, :]
            foot[f, one, :] = cx[level, f, band - 1 :, :]
            foot[faces + f, one, :] = cy[level, f, band - 1 :, :]
        mid_side[one, :] = to_lanes(outs[0][:, 0:1], 0, 128)
        x_side[one, :] = to_lanes(cx[level, 0, :, 0:1], 0, 128)


def decode(got, slots, width, flat):
    w = LOW * slots
    at = 2 * w + w // 4
    reps = 128 // (len(got) * w)
    tags = [unfold(ref[2 * w : at, :]) for ref in got]
    tag = jnp.concatenate(tags, axis=0)
    mark = lax.shift_right_arithmetic(tag, 16)

    def turned(value):
        parts = [pltpu.roll(value, 128 - r, 1) if r else value for r in range(reps)]
        return jnp.transpose(jnp.concatenate(parts, axis=0))

    for h in range(2):
        packed = jnp.concatenate([ref[h * w : (h + 1) * w, :] for ref in got], axis=0)
        size = step_size(mark[:, h : h + 1].astype(f32))
        for p, value in enumerate((upper(packed), lower(packed))):
            value = turned(value * size)
            high_part = value.astype(bf16).astype(f32)
            lines = slice((2 * h + p) * 128, (2 * h + p + 1) * 128)
            flat[0, lines, :] = high_part
            flat[1, lines, :] = value - high_part
    spots = turned((tag & 0xFFFF).astype(f32))[:width].astype(i32)
    seam = sum(seam_value(ref[at : at + KINDS, :], step_size(seam_code(t))) for t, ref in zip(tags, got))
    return spots, seam, reps


def draw_charts(charts, column, width, reps):
    edge = charts.shape[0]
    for n, k in enumerate(range(0, width, reps)):
        charts[:, n * 128 : (n + 1) * 128] = (iota((edge, 128), 0) == column[k : k + 1]).astype(f32).astype(bf16)


def spread_out(flat, line, charts, lines, sizes, width, reps, finish):
    levels, faces, band, _ = sizes
    both = ((1,), (1,))
    group = lines.shape[1] // (2 * faces * band)
    rest = faces * group * band

    def fill(g):
        for n, k in enumerate(range(0, width, reps)):
            hit = [(iota((band, 128), 0) + f * band == line[k : k + 1]).astype(f32).astype(bf16) for f in range(faces)]
            for i in range(group):
                row = (g * group + i) * width + k
                for p in range(2):
                    value = jnp.broadcast_to(flat[p, row : row + 1, :], (band, 128)).astype(bf16)
                    for f in range(faces):
                        at = p * rest + (f * group + i) * band
                        lines[g % 2, at : at + band, n * 128 : (n + 1) * 128] = hit[f] * value

    fill(0)
    for g in range(levels // group):
        field = mm(lines[g % 2], charts[...], both)
        if (g + 1) * group < levels:
            fill(g + 1)
        for i in range(group):
            at = [(f * group + i) * band for f in range(faces)]
            finish(g * group + i, [field[r : r + band] + field[r + rest : r + rest + band] for r in at])


def soon_kernel(slots, width, half, *refs):
    got = refs[:half]
    mid, mid_top, mid_side, more, more_top, more_side, seam, flat, charts, lines = refs[half:]
    _, faces, _, edge = mid.shape
    spots, seam[...], reps = decode(got, slots, width, flat)
    line, column = spots // edge, spots % edge
    draw_charts(charts, column, width, reps)

    def finish(level, adds):
        one = slice(level, level + 1)
        for f in range(faces):
            more[level, f] = mid[level, f] + adds[f]
            more_top[f, one, :] = mid_top[f, one, :] + adds[f][0:1]
        more_side[one, :] = mid_side[one, :] + to_lanes(adds[0][:, 0:1], 0, 128)

    spread_out(flat, line, charts, lines, mid.shape, width, reps, finish)


def near_kernel(slots, width, half, *refs):
    got = refs[:half]
    mid_top, mid_side, x_side, y_top, top, traded, before = refs[half : half + 7]
    below, jump, trade, flat, spots_, charts, seams = refs[half + 7 :]
    faces, levels, edge = mid_top.shape
    first, _ = spot()
    spots, seam, reps = decode(got, slots, width, flat)
    spots_[...] = spots
    seam = seam + before[...]
    band = 128 // KINDS
    again = pltpu.roll(seam, 128 - 6 * band, 1) + pltpu.roll(seam, 128 - 4 * band, 1) * seam
    seams[0] = seam
    seams[1] = again
    line, column = spots // edge, spots % edge
    draw_charts(charts, column, width, reps)
    both = ((1,), (1,))
    tops = [jnp.zeros((levels, edge), f32) for _ in range(faces)]
    side = jnp.zeros((levels, 128), f32)
    held = list(range(0, width, reps))
    step = 4
    for n in range(0, len(held), step):
        parts, sides, lefts = [], [], []
        for k in held[n : n + step]:
            value = [flat[p, pl.ds(k, levels, stride=width), :] for p in range(2)]
            parts.append(jnp.concatenate([jnp.where(line[k : k + 1] == f * band, v, 0.0) for f in range(faces) for v in value], axis=0))
            sides.append(jnp.concatenate(value, axis=0))
            lefts.append((spots[k : k + 1] == iota((128, 128), 0) * edge).astype(f32) * (iota((128, 128), 0) < band).astype(f32))
        chart = charts[:, n * 128 : (n + step) * 128]
        done = mm(jnp.concatenate(parts, axis=1).astype(bf16), chart, both)
        edge_done = mm(jnp.concatenate(sides, axis=1).astype(bf16), jnp.concatenate(lefts, axis=1).astype(bf16), both)
        for f in range(faces):
            tops[f] = tops[f] + done[2 * f * levels : (2 * f + 1) * levels] + done[(2 * f + 1) * levels : (2 * f + 2) * levels]
        side = side + edge_done[:levels] + edge_done[levels:]
    at_left = iota((levels, edge), 1) == 0
    turn = band - 1
    cross0, local0 = seam[:, 3 * band + turn : 3 * band + turn + 1], seam[:, 2 * band + turn : 2 * band + turn + 1]
    columns = (jnp.where(first, cross0, 0.0), jnp.where(first, 0.0, cross0), local0)
    for f in range(faces):
        value = mid_top[f] + tops[f] + jnp.where(at_left, columns[f], 0.0)
        below[:, f * edge : (f + 1) * edge] = top[f]
        below[:, (faces + f) * edge : (faces + f + 1) * edge] = value * y_top[f]
    below[:, 2 * faces * edge :] = pltpu.roll(traded[:, edge:], 128 - 2 * band, 1)
    jump[:, :edge] = top[faces - 1]
    jump[:, edge:] = value * y_top[faces - 1]
    lane = iota((levels, 128), 1)
    back = (iota((128, 128), 0) + iota((128, 128), 1) == 4 * band - 1).astype(f32) * (iota((128, 128), 1) < band).astype(f32)
    parts = halves(seam)
    turned = mm(parts[0], back.astype(bf16)) + mm(parts[1], back.astype(bf16))
    value = mid_side[...] + side + jnp.where(first, turned, 0.0)
    trade[...] = jnp.where(lane < band, value * x_side[...], jnp.where(lane < 2 * band, again, 0.0))


def force_kernel(reps, flat, spots, charts, seams, mid, cx, cy, result, lines):
    _, faces, band, edge = mid.shape
    width = spots.shape[0]
    first, _ = spot()
    at_left = iota((band, edge), 1) == 0
    zero_column = jnp.zeros((band, 1), f32)
    zero_row = jnp.zeros((1, edge), f32)

    def finish(level, adds):
        one = slice(level, level + 1)
        now, later = seams[0, one, :], seams[1, one, :]
        local = to_rows(now, 2 * band, band, True)
        cross = to_rows(now, 3 * band, band, True)
        columns = (jnp.where(first, cross, 0.0), jnp.where(first, 0.0, cross), local)
        faces_now = [mid[level, f] + adds[f] + jnp.where(at_left, columns[f], 0.0) for f in range(faces)]
        outs = step_level(faces_now, cx[level], cy[level], zero_column, [zero_row] * faces)
        outs[2] = outs[2] + jnp.where(at_left, to_rows(later, 0, band, True), 0.0)
        for f in range(faces):
            result[level, f] = outs[f]

    spread_out(flat, spots[...] // edge, charts, lines, mid.shape, width, reps, finish)


def final_kernel(part, below, jump, trade, traded, foot, out, hold, sent):
    levels, faces, band, edge = part.shape
    first, band_id = spot()
    last = band_id == lax.axis_size("rows") - 1
    shape_ = (band, edge)
    at_left, at_right = iota(shape_, 1) == 0, iota(shape_, 1) == edge - 1
    at_bottom, at_above = iota(shape_, 0) == band - 1, iota(shape_, 0) == band - 2

    def bottom(step):
        got = [below[:, (step * faces + f) * edge : (step * faces + f + 1) * edge] for f in range(faces)]
        far = jump[:, step * edge : (step + 1) * edge]
        seam = (jnp.where(first, far, 0.0), jnp.where(first, 0.0, got[0]), jnp.where(first, got[1], 0.0))
        return got, [jnp.where(last, s, g) for s, g in zip(seam, got)]

    got, one_back = bottom(0)
    _, now = bottom(1)
    partner = jnp.where(last, jnp.where(first, 0.0, got[2][:, 0:1]), below[:, 2 * faces * edge : 2 * faces * edge + 1])
    partner = partner * traded[:, edge + 2 * band + 1 : edge + 2 * band + 2]
    along = [foot[f] * one_back[f] for f in range(faces)]
    upward = [foot[faces + f] * one_back[f] for f in range(faces)]
    column = [along[1][:, 0:1], along[2][:, 0:1], partner]
    ends = iota((levels, edge), 1) == edge - 1
    for f in range(faces):
        flow = jnp.where(ends, column[f], pltpu.roll(along[f], edge - 1, 1))
        now[f] = now[f] + one_back[f] - along[f] - upward[f] + flow
    copies = []
    for level in range(levels):
        one = slice(level, level + 1)
        side = to_rows(trade[one, :], 0, band, False)
        cross = to_rows(trade[one, :], band, band, True)
        columns = (jnp.where(first, cross, 0.0), jnp.where(first, 0.0, cross))
        for f in range(faces):
            value = part[level, f] + jnp.where(at_bottom, now[f][one], jnp.where(at_above, upward[f][one], 0.0))
            if f < 2:
                value = value + jnp.where(at_left, columns[f], 0.0)
            else:
                value = value + jnp.where(at_right, side, 0.0)
            hold[level, f] = value
        if level % 4 == 3:
            block = pl.ds(level - 3, 4)
            copy = pltpu.make_async_copy(hold.at[block], out.at[block], sent.at[level // 4])
            copy.start()
            copies.append(copy)
    for copy in copies:
        copy.wait()


def call(kernel, outs, args, scratch=(), specs=None, room=8, grid=(), flops=0, out_specs=None):
    return pl.pallas_call(
        kernel,
        out_shape=outs,
        in_specs=specs or [VMEM] * len(args),
        out_specs=out_specs or jax.tree.map(lambda _: VMEM, outs),
        scratch_shapes=scratch,
        grid=grid,
        cost_estimate=pl.CostEstimate(flops=flops, bytes_accessed=flops, transcendentals=0) if flops else None,
        compiler_params=pltpu.CompilerParams(vmem_limit_bytes=room << 20),
    )(*args)


def shape(dims, kind=f32):
    return jax.ShapeDtypeStruct(dims, kind)


def exchange(value, apart):
    count = lax.axis_size("rows")
    return lax.ppermute(value, "rows", [(i, i ^ apart) for i in range(count)])


def issued(count):
    return [0, *reversed(range(1, count))]


def far_first(items):
    done = {}
    for n in issued(len(items)):
        done[n] = exchange(*items[n])
    return [done[n] for n in range(len(items))]


def shift_up(value):
    count = lax.axis_size("rows")
    return lax.ppermute(value, "rows", [(i, (i + count - 1) % count) for i in range(count)])


def seam_jump(value):
    count = lax.axis_size("rows")
    return lax.ppermute(value, ("face", "rows"), [(count, count - 1)])


def swap_faces(value):
    return lax.ppermute(value, "face", [(0, 1), (1, 0)])


def adjoint_pass(final_adjoint, courant_x, courant_y, ray_tiles, ray_innov, ray_dest, ray_cols):
    a, cx, cy = final_adjoint, courant_x, courant_y
    levels, faces, band, edge = a.shape
    bands = lax.axis_size("rows")
    blocks, rays, total = ray_tiles.shape[1:]
    width = ray_cols.shape[2]
    slots = max(2, 2 * blocks // bands)
    high = bands // LOW
    hbm = pl.BlockSpec(memory_space=pltpu.HBM)
    sources = (a, cx, cy, ray_tiles[0].reshape(blocks * rays, total), ray_innov[0].T, ray_dest[0].T, ray_cols[0].T)
    far = [pltpu.with_memory_space_constraint(v, pltpu.HBM) for v in sources]
    head = shape((levels, faces, 8, edge))
    near = [shape(v.shape, v.dtype) for v in sources[3:]]
    early, *heads, tiles, innov, dest, cells = call(
        edge_kernel,
        (shape((levels, edge + 128)), head, head, head, *near),
        far,
        specs=[hbm] * 7,
        scratch=[pltpu.VMEM((levels, band, 128), f32)] * 2 + [pltpu.VMEM((levels, 8, 128), f32), pltpu.SemaphoreType.DMA((10,))],
    )
    traded = swap_faces(early)
    count = bands * slots
    contrib, where_, crown = call(
        functools.partial(contrib_kernel, slots, band),
        (shape((count, total)), shape((count, 128), i32), shape((faces, levels, edge))),
        (tiles, innov, dest, cells),
    )
    each = high * slots
    rows = 2 * each + each // 4 + high * KINDS
    edge_rows = shape((faces, levels, edge))
    packed = call(
        functools.partial(pack_kernel, slots),
        (shape((rows, 128), i32),) * LOW,
        (contrib, where_, crown, *heads, traded),
        scratch=[pltpu.VMEM((bands, KINDS, 128), i32)],
    )
    got = [packed[0]] + far_first([(packed[k], k) for k in range(1, LOW)])
    side = shape((levels, 128))
    field = shape(a.shape)
    groups = levels // 4
    mid, mid_top, mid_side, x_side, foot, first_rows, y_top, cx_in, cy_in = call(
        mid_kernel,
        (field, edge_rows, side, side, shape((2 * faces, levels, edge)), edge_rows, edge_rows, field, field),
        (*far[:3], traded),
        specs=[hbm] * 3 + [VMEM],
        scratch=[pltpu.VMEM(a.shape, f32), pltpu.SemaphoreType.DMA((3 * groups,))],
        room=16,
    )
    each = LOW * slots
    rows = 2 * each + each // 4 + KINDS
    sends = call(
        functools.partial(regroup_kernel, slots, high, levels),
        (shape((rows, 128), i32),) * high,
        (*got, mid_side),
    )
    arrived = [sends[0]] + far_first([(sends[m], m * LOW) for m in range(1, high)])
    half = high // 2
    reps = 128 // (half * each)
    lines = 2 * levels * faces * band
    deep = width // reps * 128
    kept = [shape((2, total, 128)), shape((edge, deep), bf16)]
    spread_lines = pltpu.VMEM((2, lines // 2, deep), bf16)
    mid, mid_top, mid_side, before = call(
        functools.partial(soon_kernel, slots, width, half),
        (field, edge_rows, side, side),
        (*arrived[:half], mid, mid_top, mid_side),
        scratch=[pltpu.VMEM(v.shape, v.dtype) for v in kept] + [spread_lines],
        room=28,
        flops=2 * lines * deep * edge,
    )
    below, jump, trade, flat, spots, charts, seams = call(
        functools.partial(near_kernel, slots, width, half),
        (
            shape((levels, 2 * faces * edge + 128)),
            shape((levels, 2 * edge)),
            side,
            kept[0],
            shape((width, 128), i32),
            kept[1],
            shape((2, levels, 128)),
        ),
        (*arrived[half:], mid_top, mid_side, x_side, y_top, first_rows, traded, before),
        room=16,
    )
    below_got = shift_up(below)
    jump_got = seam_jump(jump)
    trade_got = swap_faces(trade)
    part = call(
        functools.partial(force_kernel, reps),
        field,
        (flat, spots, charts, seams, mid, cx_in, cy_in),
        scratch=[spread_lines],
        room=28,
        flops=2 * lines * deep * edge,
    )
    return call(
        final_kernel,
        field,
        (part, below_got, jump_got, trade_got, traded, foot),
        scratch=[pltpu.VMEM(a.shape, f32), pltpu.SemaphoreType.DMA((groups,))],
        out_specs=hbm,
    )


def solution(mesh):
    placed = (
        P(None, "face", "rows", None),
        P(None, "face", "rows", None),
        P(None, "face", "rows", None),
        P("face", "rows", None, None),
        P("face", "rows", None),
        P("face", "rows", None),
        P("face", "rows", None),
    )
    return jax.shard_map(
        adjoint_pass,
        mesh=mesh,
        in_specs=placed,
        out_specs=P(None, "face", "rows", None),
        check_vma=False,
    )
```
